32 devices in a mesh: groups: 2 (over y), section: 4 (over x, core), dp: 4 (over z).
Axes of the slice: x: 2, y: 2, z: 4, core: 2. Of those that a mesh axis runs over, the one named last changes fastest.
Arguments:
- patches: bfloat16 [8192, 1024], P(('groups', 'dp'), 'section'), parts along dimension 0, may hold values from -6 to 6
- clip_slot: int32 [256], P('groups'), parts along dimension 0, may hold values from 0 to 127, each once
- w_qkv: bfloat16 [4, 1024, 1536], P('section'), may hold values from -0.1875 to 0.1875
- w_out: bfloat16 [4, 512, 1024], P('section'), may hold values from -0.25 to 0.25
- w_up: bfloat16 [4, 1024, 2048], P('section'), may hold values from -0.1875 to 0.1875
- w_down: bfloat16 [4, 2048, 1024], P('section'), may hold values from -0.125 to 0.125
- norm_gains: float32 [4, 2, 1024], P('section'), may hold values from 0.5 to 1.5
- level_one_weight: bfloat16 [3, 1024, 1024], P(None, 'section'), may hold values from -0.109375 to 0.109375
- level_two_weight: bfloat16 [3, 1024, 1024], P(None, 'section'), may hold values from -0.109375 to 0.109375
- head_weight: bfloat16 [1024, 22], P('section'), may hold values from -0.1875 to 0.1875
Outputs:
- level_one_heads: float32 [256, 22], P(('groups', 'dp')), parts along dimension 0
- level_two_heads: float32 [128, 22], P(('groups', 'dp')), parts along dimension 0
The draws below stay inside these ranges and needn't reach their ends.
There are 2 independent parts, one for each index of `groups`. The reference program is written for one: setup_inputs(seed, part) draws one part's arguments, and reference() takes and returns one part's arrays. A program takes and returns all parts, laid end to end along the dimension named above; an argument that names none is the same for every part. Nothing has to cross between parts.
Inputs may be any that keep to these rules, and one draw needn't show every extreme that they name: clip_slot is a permutation: every slot of the window holds exactly one clip.
All inputs are finite; a program needn't handle non-finite values.
Results may differ from the reference program's by a relative error of at most 0.035.
Values may be sent and summed in bfloat16 or wider, within the bound.
A program may use at most 64 MiB of HBM per device.

```python
import jax
import jax.numpy as jnp
from jax import lax

D = 1024
HEADS = 8
HEAD = 64
HID = 2048
HO = 22
PATCHES = 16
TUB_CLIP = 2
CLIP_TOK = 32
LAYERS = 4
N_CLIPS = 128


def levels(key, shape, split, low, largest):
    gain = 1.0
    for dim, blocks in split:
        draws = jax.random.uniform(jax.random.fold_in(jax.random.fold_in(key, 6), dim), (blocks,), jnp.float32, low / len(split), largest / len(split))
        gain = gain * jnp.repeat(jnp.exp(draws), shape[dim] // blocks).reshape((-1,) + (1,) * (len(shape) - 1 - dim))
    return gain


def noise(rng, extent, deviation, limit, cuts=(), kind=jnp.bfloat16):
    gain = levels(rng, extent, cuts, -0.22, 0.18) if cuts else 1.0
    array = jax.random.normal(rng, extent, jnp.float32) * deviation * gain
    return jnp.minimum(jnp.maximum(array, -limit), limit).astype(kind)


def setup_inputs(seed: int = 0, part: int = 0) -> dict:
    arg_keys = jax.random.split(jax.random.key(seed), 11)
    own_keys = jax.random.split(jax.random.fold_in(arg_keys[10], part), 11)
    return {
        "patches": noise(own_keys[0], (N_CLIPS * CLIP_TOK, D), 1.0, 6.0, ((0, 4), (1, 4))),
        "clip_slot": jax.random.permutation(own_keys[1], N_CLIPS).astype(jnp.int32),
        "w_qkv": noise(arg_keys[2], (LAYERS, D, 3 * HEADS * HEAD), D ** -0.5, 0.1875, ((0, 4),)),
        "w_out": noise(arg_keys[3], (LAYERS, HEADS * HEAD, D), (HEADS * HEAD) ** -0.5, 0.25, ((0, 4),)),
        "w_up": noise(arg_keys[4], (LAYERS, D, HID), D ** -0.5, 0.1875, ((0, 4),)),
        "w_down": noise(arg_keys[5], (LAYERS, HID, D), HID ** -0.5, 0.125, ((0, 4),)),
        "norm_gains": jnp.clip(1.0 + 0.1 * jax.random.normal(arg_keys[6], (LAYERS, 2, D), jnp.float32), 0.5, 1.5),
        "level_one_weight": noise(arg_keys[7], (3, D, D), (3 * D) ** -0.5, 0.109375, ((1, 4),)),
        "level_two_weight": noise(arg_keys[8], (3, D, D), (3 * D) ** -0.5, 0.109375, ((1, 4),)),
        "head_weight": noise(arg_keys[9], (D, HO), D ** -0.5, 0.1875, ((0, 4),)),
    }


EPSILON = 1e-05

def layer_norm(values, scaling):
    average = lax.optimization_barrier(jnp.mean(values, axis=-1, keepdims=True))
    centred = values - average
    spread = lax.optimization_barrier(jnp.mean(centred * centred, axis=-1, keepdims=True))
    return centred * lax.rsqrt(spread + EPSILON) * scaling

def head_norm(values):
    return values * lax.rsqrt(lax.optimization_barrier(jnp.mean(values * values, axis=-1, keepdims=True)) + EPSILON)

def vit_layer(stream, w_qkv, w_out, w_up, w_down, gains, clip_tok, head_count, head_size):
    row_count = stream.shape[0]
    clip_count = row_count // clip_tok
    residual = stream.astype(jnp.float32)
    normed = layer_norm(residual, gains[0]).astype(jnp.bfloat16)
    projected = jnp.dot(normed, w_qkv, preferred_element_type=jnp.float32)
    projected = projected.reshape(clip_count, clip_tok, 3, head_count, head_size)
    queries = head_norm(projected[:, :, 0]).astype(jnp.bfloat16)
    key_rows = head_norm(projected[:, :, 1]).astype(jnp.bfloat16)
    value_rows = projected[:, :, 2].astype(jnp.bfloat16)
    scores = jnp.einsum('cqhd,ckhd->chqk', queries.astype(jnp.float32), key_rows.astype(jnp.float32)) * head_size ** (-0.5)
    exponent = jnp.exp(scores)
    attention_weights = (exponent / lax.optimization_barrier(jnp.sum(exponent, axis=-1, keepdims=True))).astype(jnp.bfloat16)
    mixture = jnp.einsum('chqk,ckhd->cqhd', attention_weights.astype(jnp.float32), value_rows.astype(jnp.float32))
    mixture = mixture.astype(jnp.bfloat16).reshape(row_count, head_count * head_size)
    residual = residual + jnp.dot(mixture, w_out, preferred_element_type=jnp.float32)
    normed_b = layer_norm(residual, gains[1]).astype(jnp.bfloat16)
    hidden = jax.nn.gelu(jnp.dot(normed_b, w_up, preferred_element_type=jnp.float32), approximate=True).astype(jnp.bfloat16)
    residual = residual + jnp.dot(hidden, w_down, preferred_element_type=jnp.float32)
    return residual.astype(jnp.bfloat16)

def pyramid_level(inputs, weight):
    padded = jnp.concatenate([jnp.zeros((1, inputs.shape[1]), inputs.dtype), inputs], axis=0)
    length = inputs.shape[0]
    earlier_rows = padded[0:length:2]
    middle = padded[1:length + 1:2]
    later_rows = padded[2::2]
    summed = jnp.dot(earlier_rows, weight[0], preferred_element_type=jnp.float32)
    summed = summed + jnp.dot(middle, weight[1], preferred_element_type=jnp.float32)
    summed = summed + jnp.dot(later_rows, weight[2], preferred_element_type=jnp.float32)
    return jax.nn.gelu(summed, approximate=True).astype(jnp.bfloat16)

def reference(patches, clip_slot, w_qkv, w_out, w_up, w_down, norm_gains, level_one_weight, level_two_weight, head_weight):

    def advance(stream, layer_weights):
        return (vit_layer(stream, *layer_weights, CLIP_TOK, HEADS, HEAD), None)
    stream, _ = lax.scan(advance, patches, (w_qkv, w_out, w_up, w_down, norm_gains))
    tube_rows = stream.astype(jnp.float32).reshape(N_CLIPS * TUB_CLIP, PATCHES, D)
    pooled = lax.optimization_barrier(jnp.mean(tube_rows, axis=1)).astype(jnp.bfloat16)
    position = (clip_slot[:, None] * TUB_CLIP + jnp.arange(TUB_CLIP, dtype=jnp.int32)[None, :]).reshape(-1)
    film_rows = jnp.zeros_like(pooled).at[position].set(pooled)
    level_one = pyramid_level(film_rows, level_one_weight)
    level_two = pyramid_level(level_one, level_two_weight)
    level_one_heads = jnp.dot(level_one, head_weight, preferred_element_type=jnp.float32)
    level_two_heads = jnp.dot(level_two, head_weight, preferred_element_type=jnp.float32)
    return (level_one_heads, level_two_heads)
```

```python
import functools

import jax
import jax.numpy as jnp
from jax import lax
from jax.experimental import pallas as pl
from jax.experimental.pallas import tpu as pltpu
from jax.sharding import PartitionSpec as P

HEADS = 8
HEAD = 64
PATCHES = 16
TUB_CLIP = 2
EPSILON = 1e-05
UNIT_ROWS = 128
ROW_BLOCK = 128
CHUNK = 512
COLUMNS = 256
STOP = 9
MESH = pl.DeviceIdType.MESH
F32 = jnp.float32
BF16 = jnp.bfloat16


def dot(a, b):
    return jnp.dot(a, b, preferred_element_type=F32)


def dot_nt(a, b):
    return lax.dot_general(a, b, (((1,), (1,)), ((), ())), preferred_element_type=F32)


def gelu(values):
    return jax.nn.gelu(values, approximate=True)


def gelu_rounded(values):
    x = values.astype(BF16)
    inner = x * (x * x * 0.035677408136300125 + 0.7978845608028654)
    return x * (jnp.tanh(inner) * 0.5 + 0.5)


def iota(shape, dim):
    return lax.broadcasted_iota(jnp.int32, shape, dim)


def centre(values, scaling):
    average = jnp.mean(values, axis=-1, keepdims=True)
    square = jnp.mean(values * values, axis=-1, keepdims=True)
    spread = jnp.maximum(square - average * average, 0.0) + EPSILON
    return ((values - average) * scaling).astype(BF16), spread


def backbone_layer(stream, gains, v_qkv, v_out, v_up, emit):
    inner = v_out.shape[0]
    hidden = v_up.shape[1]
    pair = 2 * HEAD
    clip = PATCHES * TUB_CLIP
    rows = stream.shape[0]
    group = min(256, inner)
    normed, spread = centre(stream, gains[0, 0:1])
    raw = []
    for start in range(0, inner, group):
        raw.append(
            (
                dot(normed, v_qkv[:, start : start + group]),
                dot(normed, v_qkv[:, inner + start : inner + start + group]),
            )
        )
    scale = lax.rsqrt(spread)
    values = [
        (dot(normed, v_qkv[:, 2 * inner + start : 2 * inner + start + group]) * scale).astype(BF16)
        for start in range(0, inner, group)
    ]
    same = iota((group, group), 0) // HEAD == iota((group, group), 1) // HEAD
    averaging = jnp.where(same, 1.0 / HEAD, 0.0).astype(BF16)
    floor = EPSILON * spread

    def head_scale(part):
        return part * lax.rsqrt(dot((part * part).astype(BF16), averaging) + floor)

    cross = (2 * rows, pair)
    own = (iota(cross, 0) < rows) == (iota(cross, 1) < HEAD)
    own_bf = jnp.where(own, 1.0, 0.0).astype(BF16)
    square = (rows, 2 * rows)
    same_clip = iota(square, 0) // clip == (iota(square, 1) % rows) // clip
    mixed = []
    for (raw_q, raw_k), value in zip(raw, values):
        query = (head_scale(raw_q) * HEAD**-0.5).astype(BF16)
        key = head_scale(raw_k).astype(BF16)
        for lane in range(0, group, pair):
            q = query[:, lane : lane + pair]
            k = key[:, lane : lane + pair]
            v = value[:, lane : lane + pair]
            k2 = jnp.concatenate([k, k], axis=0) * own_bf
            v2 = jnp.concatenate([v, v], axis=0) * own_bf
            weights = jnp.where(same_clip, jnp.exp(dot_nt(q, k2)), 0.0).astype(BF16)
            both = dot(weights, jnp.concatenate([v2, own_bf], axis=1))
            mixed.append((both[:, :pair] / both[:, pair:]).astype(BF16))
    residual = stream + dot(jnp.concatenate(mixed, axis=1), v_out[...])
    normed_b, spread_b = centre(residual, gains[0, 1:2])
    scale_b = lax.rsqrt(spread_b)
    parts = [
        gelu_rounded(dot(normed_b, v_up[:, start : start + CHUNK]) * scale_b)
        for start in range(0, hidden, CHUNK)
    ]
    emit(residual, jnp.concatenate(parts, axis=1))


def kernel(
    sections,
    shards,
    patches,
    clip_slot,
    w_qkv,
    w_out,
    w_up,
    w_down,
    gains,
    one_weight,
    two_weight,
    head_weight,
    heads,
    v_qkv,
    v_out,
    v_up,
    v_down,
    v_one,
    v_two,
    inbuf,
    outbuf,
    pooled_out,
    film_in,
    one_out,
    one_in,
    two_out,
    two_in,
    part_out,
    part_in,
    own_head,
    all_head,
    weight_sem,
    gather_send,
    arrive,
    hop_send,
    film_send,
    film_recv,
    ex_send,
    ex_recv,
):
    section = lax.axis_index("section")
    shard = lax.axis_index("dp")
    last = sections - 1
    units, _, unit_rows, channels = outbuf.shape
    width = sections * channels
    tubes_unit = unit_rows // PATCHES
    is_last = lax.div(section + 1, sections)
    outputs = head_weight.shape[0]
    loads = [
        pltpu.make_async_copy(source, target, weight_sem.at[index])
        for index, (source, target) in enumerate(
            (
                (w_qkv.at[0], v_qkv),
                (w_out.at[0], v_out),
                (w_up.at[0], v_up),
                (w_down.at[0], v_down),
                (one_weight, v_one),
                (two_weight, v_two),
            )
        )
    ]
    for load in loads:
        load.start()
    own_head[...] = jnp.zeros(own_head.shape, BF16)
    own_head[0:outputs] = head_weight[...]

    barrier = pltpu.get_barrier_semaphore()
    for ds in range(sections):
        for dd in range(shards):
            if ds or dd:
                pl.semaphore_signal(
                    barrier,
                    inc=1,
                    device_id={
                        "section": lax.rem(section + ds, sections),
                        "dp": lax.rem(shard + dd, shards),
                    },
                    device_id_type=MESH,
                )
    pl.semaphore_wait(barrier, sections * shards - 1)

    def patch_rows(u):
        return patches.at[pl.ds(pl.multiple_of(u * unit_rows, unit_rows), unit_rows)]

    def patch_copy(u):
        return pltpu.make_async_remote_copy(
            src_ref=patch_rows(u),
            dst_ref=inbuf.at[u, section],
            send_sem=gather_send.at[u],
            recv_sem=arrive.at[u],
            device_id={"section": 0},
            device_id_type=MESH,
        )

    def each_unit(body):
        def step(u, carry):
            body(u)
            return carry

        lax.fori_loop(0, units, step, 0)

    @pl.when(section > 0)
    def _():
        each_unit(lambda u: patch_copy(u).start())

    @pl.when(section == 0)
    def _():
        each_unit(
            lambda u: pltpu.make_async_copy(patch_rows(u), inbuf.at[u, 0], arrive.at[u]).start()
        )

    def hop(u, block):
        slot = u + is_last * units
        return pltpu.make_async_remote_copy(
            src_ref=outbuf.at[u, block],
            dst_ref=inbuf.at[slot, block],
            send_sem=hop_send.at[u],
            recv_sem=arrive.at[slot],
            device_id={"section": section + 1 - 2 * is_last},
            device_id_type=MESH,
        )

    def arrival(slot):
        return pltpu.make_async_copy(inbuf.at[slot], inbuf.at[slot], arrive.at[slot])

    tubes_own = units * tubes_unit
    tubes_pair = 2 * tubes_unit
    batches = ((0, tubes_own - tubes_pair), (tubes_own - tubes_pair, tubes_pair))
    film_targets = [
        (target, step)
        for target in range(sections)
        for step in range(shards)
        if not (target == last and step == 0)
    ]

    def film_copy(batch, target, step):
        start, count = batches[batch]
        return pltpu.make_async_remote_copy(
            src_ref=pooled_out.at[target, pl.ds(start, count)],
            dst_ref=film_in.at[shard, pl.ds(start, count)],
            send_sem=film_send.at[batch, target, step],
            recv_sem=film_recv.at[batch, shard],
            device_id={"section": target, "dp": lax.rem(shard + step, shards)},
            device_id_type=MESH,
        )

    def film_arrival(batch, source):
        start, count = batches[batch]
        return pltpu.make_async_copy(
            film_in.at[source, pl.ds(start, count)],
            film_in.at[source, pl.ds(start, count)],
            film_recv.at[batch, source],
        )

    pooling_shape = (tubes_pair, 2 * unit_rows)
    pooling = jnp.where(
        iota(pooling_shape, 1) // PATCHES == iota(pooling_shape, 0), 1.0 / PATCHES, 0.0
    ).astype(BF16)

    def pool(p):
        rows = pl.ds(pl.multiple_of(p * tubes_pair, tubes_pair), tubes_pair)
        for target in range(sections):
            both = jnp.concatenate([outbuf[2 * p, target], outbuf[2 * p + 1, target]], axis=0)
            pooled = dot(pooling, both).astype(BF16)
            if target == last:
                film_in[shard, rows] = pooled
            else:
                pooled_out[target, rows] = pooled
            if target == last:
                pooled_out[target, rows] = pooled

    for load in loads[:4]:
        load.wait()

    blocks = max(1, COLUMNS // channels)

    def run_unit(u):
        arrival(u).wait()
        stream = jnp.concatenate([inbuf[u, source] for source in range(sections)], axis=1)

        def emit(residual, gated):
            for first in range(0, sections, blocks):
                columns = slice(first * channels, (first + blocks) * channels)
                result = (residual[:, columns] + dot(gated, v_down[:, columns])).astype(BF16)
                for block in range(blocks):
                    outbuf[u, first + block] = result[:, block * channels : (block + 1) * channels]
                    hop(u, first + block).start()

        backbone_layer(stream.astype(F32), gains, v_qkv, v_out, v_up, emit)

        @pl.when((section == last) & (u % 2 == 1))
        def _():
            pool(u // 2)
            for batch, unit in ((0, units - 3), (1, units - 1)):

                @pl.when((u == unit) if STOP >= 1 else False)
                def _():
                    for target, step in film_targets:
                        film_copy(batch, target, step).start()

    each_unit(run_unit)

    def exchange(stage, outgoing, incoming):
        copies = []
        for step in range(sections - 1, 0, -1):
            target = lax.rem(section + step, sections)
            copies.append(
                pltpu.make_async_remote_copy(
                    src_ref=outgoing(target),
                    dst_ref=incoming.at[section],
                    send_sem=ex_send.at[stage, step],
                    recv_sem=ex_recv.at[stage, section],
                    device_id={"section": target},
                    device_id_type=MESH,
                )
            )
        for copy in copies:
            copy.start()

        def arrivals():
            for step in range(1, sections):
                source = lax.rem(section + step, sections)
                pltpu.make_async_copy(
                    incoming.at[source], incoming.at[source], ex_recv.at[stage, source]
                ).wait()

        def sent():
            for copy in copies:
                copy.wait_send()

        return arrivals, sent

    head_arrivals, head_sent = exchange(3, lambda target: own_head, all_head)
    all_head[section] = own_head[...]

    def finish():
        head_arrivals()
        head_sent()

        @pl.when(section > 0)
        def _():
            each_unit(lambda u: patch_copy(u).wait_send())

        each_unit(lambda u: pltpu.make_async_copy(outbuf.at[u], outbuf.at[u], hop_send.at[u]).wait())

        @pl.when(section == last - 1)
        def _():
            each_unit(lambda u: arrival(units + u).wait())

        @pl.when((section == last) if STOP >= 1 else False)
        def _():
            for batch in (0, 1):
                for target, step in film_targets:
                    film_copy(batch, target, step).wait_send()

    loads[4].wait()
    loads[5].wait()
    if STOP < 9:
        heads[...] = jnp.zeros(heads.shape, F32)
    if STOP == 0:
        return finish()

    for batch in (0, 1):

        @pl.when(section < last)
        def _():
            film_arrival(batch, shard).wait()

        for step in range(1, shards):
            film_arrival(batch, lax.rem(shard + step, shards)).wait()
    if STOP == 1:
        return finish()

    tubes = shards * tubes_own
    pooled = film_in[...].reshape(tubes, channels)
    clips = tubes // TUB_CLIP
    spread_shape = (clips, tubes)
    spread = jnp.where(iota(spread_shape, 1) // TUB_CLIP == iota(spread_shape, 0), 1.0, 0.0)
    slots = jnp.broadcast_to(clip_slot[...].astype(F32), (8, clips)).astype(BF16)
    position = TUB_CLIP * dot(slots, spread.astype(BF16))[0:1]
    position = position + (iota((1, tubes), 1) % TUB_CLIP).astype(F32)

    two_rows = two_out.shape[0]
    one_rows = 3 * two_rows
    row = iota((one_rows, 1), 0)
    level_index = 2 * (shard * two_rows + row % two_rows) + row // two_rows - 1
    taps = []
    for tap in range(3):
        wanted = (2 * level_index + tap - 1).astype(F32)
        selector = jnp.where(position == wanted, 1.0, 0.0).astype(BF16)
        taps.append(dot(selector, pooled).astype(BF16))

    def conv(parts, weight):
        total = dot(parts[0], weight[0])
        for tap in (1, 2):
            total = total + dot(parts[tap], weight[tap])
        return total.astype(BF16)

    def total(incoming):
        value = incoming[0].astype(F32)
        for source in range(1, sections):
            value = value + incoming[source].astype(F32)
        return value

    partial = conv(taps, v_one)
    for target in range(sections):
        one_out[target] = partial[:, target * channels : (target + 1) * channels]
    arrivals, one_sent = exchange(0, lambda target: one_out.at[target], one_in)
    one_in[section] = one_out[section]
    finish()
    arrivals()
    one = gelu(total(one_in)).astype(BF16)

    natural = 2 * two_rows
    order = (natural, one_rows)
    chosen = iota(order, 1) == (1 + iota(order, 0) % 2) * two_rows + iota(order, 0) // 2
    one_natural = dot(jnp.where(chosen, 1.0, 0.0).astype(BF16), one).astype(BF16)
    two_out[...] = conv([one[block * two_rows : (block + 1) * two_rows] for block in range(3)], v_two)
    two_arrivals, two_sent = exchange(1, lambda target: two_out, two_in)
    part_out[...] = dot_nt(own_head[...], one_natural)
    part_arrivals, part_sent = exchange(2, lambda target: part_out, part_in)
    two_in[section] = two_out[...]
    part_in[section] = part_out[...]
    one_sent()
    two_arrivals()
    two = gelu(total(two_in)).astype(BF16)
    every_head = jnp.concatenate([all_head[source] for source in range(sections)], axis=1)
    level_two = dot_nt(two, every_head)
    part_arrivals()
    heads[0 : own_head.shape[0], 0:natural] = total(part_in)
    heads[own_head.shape[0] :, 0 : own_head.shape[0]] = level_two
    two_sent()
    part_sent()


def split_heads(heads, head_one, head_two):
    outputs, natural = head_one.shape
    two_rows = head_two.shape[0]
    head_one[...] = heads[0:outputs, 0:natural]
    head_two[...] = heads[heads.shape[0] - two_rows :, 0:outputs]


def on_device(
    patches,
    clip_slot,
    w_qkv,
    w_out,
    w_up,
    w_down,
    norm_gains,
    level_one_weight,
    level_two_weight,
    head_weight,
):
    sections = lax.axis_size("section")
    shards = lax.axis_size("dp")
    rows, channels = patches.shape
    width = channels * sections
    unit_rows = UNIT_ROWS
    units = rows // unit_rows
    tubes_unit = unit_rows // PATCHES
    outputs = head_weight.shape[1]
    one_rows = rows // PATCHES // 2
    two_rows = one_rows // 2
    vmem = pl.BlockSpec(memory_space=pltpu.VMEM)
    anywhere = pl.BlockSpec(memory_space=pl.ANY)
    dma = pltpu.SemaphoreType.DMA
    head_rows = -(-outputs // 16) * 16
    heads = pl.pallas_call(
        functools.partial(kernel, sections, shards),
        out_shape=jax.ShapeDtypeStruct((head_rows + two_rows, 128), F32),
        in_specs=[anywhere, vmem] + [anywhere] * 4 + [vmem] + [anywhere] * 2 + [vmem],
        out_specs=vmem,
        scratch_shapes=[
            pltpu.VMEM(w_qkv.shape[1:], BF16),
            pltpu.VMEM(w_out.shape[1:], BF16),
            pltpu.VMEM(w_up.shape[1:], BF16),
            pltpu.VMEM(w_down.shape[1:], BF16),
            pltpu.VMEM(level_one_weight.shape, BF16),
            pltpu.VMEM(level_two_weight.shape, BF16),
            pltpu.VMEM((2 * units, sections, unit_rows, channels), BF16),
            pltpu.VMEM((units, sections, unit_rows, channels), BF16),
            pltpu.VMEM((sections, units * tubes_unit, channels), BF16),
            pltpu.VMEM((shards, units * tubes_unit, channels), BF16),
            pltpu.VMEM((sections, 3 * two_rows, channels), BF16),
            pltpu.VMEM((sections, 3 * two_rows, channels), BF16),
            pltpu.VMEM((two_rows, width), BF16),
            pltpu.VMEM((sections, two_rows, width), BF16),
            pltpu.VMEM((head_rows, 2 * two_rows), F32),
            pltpu.VMEM((sections, head_rows, 2 * two_rows), F32),
            pltpu.VMEM((head_rows, channels), BF16),
            pltpu.VMEM((sections, head_rows, channels), BF16),
            dma((6,)),
            dma((units,)),
            dma((2 * units,)),
            dma((units,)),
            dma((2, sections, shards)),
            dma((2, shards)),
            dma((4, sections)),
            dma((4, sections)),
        ],
        compiler_params=pltpu.CompilerParams(
            collective_id=0, has_side_effects=True, vmem_limit_bytes=60 * 1024 * 1024
        ),
    )(
        patches,
        clip_slot.reshape(1, -1),
        w_qkv,
        w_out,
        w_up,
        w_down,
        norm_gains,
        level_one_weight,
        level_two_weight,
        head_weight.T,
    )
    head_one, head_two = pl.pallas_call(
        split_heads,
        out_shape=(
            jax.ShapeDtypeStruct((outputs, one_rows), F32),
            jax.ShapeDtypeStruct((two_rows, outputs), F32),
        ),
        in_specs=[vmem],
        out_specs=(vmem, vmem),
    )(heads)
    return head_one.T, head_two


def solution(mesh):
    return jax.shard_map(
        on_device,
        mesh=mesh,
        in_specs=(
            P(("groups", "dp"), "section"),
            P("groups"),
            P("section", None, None),
            P("section", None, None),
            P("section", None, None),
            P("section", None, None),
            P("section", None, None),
            P(None, "section", None),
            P(None, "section", None),
            P("section", None),
        ),
        out_specs=(P(("groups", "dp"), None), P(("groups", "dp"), None)),
        check_vma=False,
    )
```

```python
import functools

import jax
import jax.numpy as jnp
from jax import lax
from jax.experimental import pallas as pl
from jax.experimental.pallas import tpu as pltpu
from jax.sharding import PartitionSpec as P

HEADS = 8
HEAD = 64
PATCHES = 16
TUB_CLIP = 2
EPSILON = 1e-05
UNIT_ROWS = 128
ROW_BLOCK = 128
CHUNK = 512
COLUMNS = 256
STOP = 9
MESH = pl.DeviceIdType.MESH
F32 = jnp.float32
BF16 = jnp.bfloat16


def dot(a, b):
    return jnp.dot(a, b, preferred_element_type=F32)


def dot_nt(a, b):
    return lax.dot_general(a, b, (((1,), (1,)), ((), ())), preferred_element_type=F32)


def gelu(values):
    return jax.nn.gelu(values, approximate=True)


def gelu_rounded(values):
    x = values.astype(BF16)
    inner = x * (x * x * 0.035677408136300125 + 0.7978845608028654)
    return x * (jnp.tanh(inner) * 0.5 + 0.5)


def iota(shape, dim):
    return lax.broadcasted_iota(jnp.int32, shape, dim)


def centre(values, scaling):
    average = jnp.mean(values, axis=-1, keepdims=True)
    square = jnp.mean(values * values, axis=-1, keepdims=True)
    spread = jnp.maximum(square - average * average, 0.0) + EPSILON
    return ((values - average) * scaling).astype(BF16), spread


def backbone_layer(stream, gains, v_qkv, v_out, v_up, emit):
    inner = v_out.shape[0]
    hidden = v_up.shape[1]
    pair = 2 * HEAD
    clip = PATCHES * TUB_CLIP
    rows = stream.shape[0]
    group = min(256, inner)
    normed, spread = centre(stream, gains[0, 0:1])
    raw = []
    for start in range(0, inner, group):
        raw.append(
            (
                dot(normed, v_qkv[:, start : start + group]),
                dot(normed, v_qkv[:, inner + start : inner + start + group]),
            )
        )
    scale = lax.rsqrt(spread)
    values = [
        (dot(normed, v_qkv[:, 2 * inner + start : 2 * inner + start + group]) * scale).astype(BF16)
        for start in range(0, inner, group)
    ]
    same = iota((group, group), 0) // HEAD == iota((group, group), 1) // HEAD
    averaging = jnp.where(same, 1.0 / HEAD, 0.0).astype(BF16)
    floor = EPSILON * spread

    def head_scale(part):
        return part * lax.rsqrt(dot((part * part).astype(BF16), averaging) + floor)

    cross = (2 * rows, pair)
    own = (iota(cross, 0) < rows) == (iota(cross, 1) < HEAD)
    own_bf = jnp.where(own, 1.0, 0.0).astype(BF16)
    square = (rows, 2 * rows)
    same_clip = iota(square, 0) // clip == (iota(square, 1) % rows) // clip
    mixed = []
    for (raw_q, raw_k), value in zip(raw, values):
        query = (head_scale(raw_q) * HEAD**-0.5).astype(BF16)
        key = head_scale(raw_k).astype(BF16)
        for lane in range(0, group, pair):
            q = query[:, lane : lane + pair]
            k = key[:, lane : lane + pair]
            v = value[:, lane : lane + pair]
            k2 = jnp.concatenate([k, k], axis=0) * own_bf
            v2 = jnp.concatenate([v, v], axis=0) * own_bf
            weights = jnp.where(same_clip, jnp.exp(dot_nt(q, k2)), 0.0).astype(BF16)
            both = dot(weights, jnp.concatenate([v2, own_bf], axis=1))
            mixed.append((both[:, :pair] / both[:, pair:]).astype(BF16))
    residual = stream + dot(jnp.concatenate(mixed, axis=1), v_out[...])
    normed_b, spread_b = centre(residual, gains[0, 1:2])
    scale_b = lax.rsqrt(spread_b)
    parts = [
        gelu_rounded(dot(normed_b, v_up[:, start : start + CHUNK]) * scale_b)
        for start in range(0, hidden, CHUNK)
    ]
    emit(residual, jnp.concatenate(parts, axis=1))


def kernel(
    sections,
    shards,
    patches,
    clip_slot,
    w_qkv,
    w_out,
    w_up,
    w_down,
    gains,
    one_weight,
    two_weight,
    head_weight,
    heads,
    v_qkv,
    v_out,
    v_up,
    v_down,
    v_one,
    v_two,
    patch_buf,
    inbuf,
    outbuf,
    pooled_out,
    film_in,
    one_out,
    one_in,
    two_out,
    two_in,
    part_out,
    part_in,
    own_head,
    all_head,
    weight_sem,
    gather_send,
    arrive,
    hop_send,
    film_send,
    film_recv,
    ex_send,
    ex_recv,
):
    section = lax.axis_index("section")
    shard = lax.axis_index("dp")
    last = sections - 1
    units, _, unit_rows, channels = outbuf.shape
    width = sections * channels
    tubes_unit = unit_rows // PATCHES
    outputs = head_weight.shape[0]
    loads = [
        pltpu.make_async_copy(source, target, weight_sem.at[index])
        for index, (source, target) in enumerate(
            (
                (w_qkv.at[0], v_qkv),
                (w_out.at[0], v_out),
                (w_up.at[0], v_up),
                (w_down.at[0], v_down),
                (one_weight, v_one),
                (two_weight, v_two),
            )
        )
    ]
    def each_unit(body):
        def step(u, carry):
            body(u)
            return carry

        lax.fori_loop(0, units, step, 0)

    def patch_rows(u):
        return pl.ds(pl.multiple_of(u * unit_rows, unit_rows), unit_rows)

    patch_load = pltpu.make_async_copy(patches, patch_buf, weight_sem.at[6])

    @pl.when(section > 0)
    def _():
        patch_load.start()

    @pl.when(section == 0)
    def _():
        each_unit(
            lambda u: pltpu.make_async_copy(
                patches.at[patch_rows(u)], inbuf.at[u, 0], arrive.at[u]
            ).start()
        )

    for load in loads[:4]:
        load.start()
    own_head[...] = jnp.zeros(own_head.shape, BF16)
    own_head[0:outputs] = head_weight[...]

    barrier = pltpu.get_barrier_semaphore()
    for ds in range(sections):
        for dd in range(shards):
            if ds or dd:
                pl.semaphore_signal(
                    barrier,
                    inc=1,
                    device_id={
                        "section": lax.rem(section + ds, sections),
                        "dp": lax.rem(shard + dd, shards),
                    },
                    device_id_type=MESH,
                )
    pl.semaphore_wait(barrier, sections * shards - 1)

    def patch_copy(u):
        return pltpu.make_async_remote_copy(
            src_ref=patch_buf.at[patch_rows(u)],
            dst_ref=inbuf.at[u, section],
            send_sem=gather_send.at[u],
            recv_sem=arrive.at[u],
            device_id={"section": 0},
            device_id_type=MESH,
        )

    @pl.when(section > 0)
    def _():
        patch_load.wait()
        each_unit(lambda u: patch_copy(u).start())

    def hop(u):
        return pltpu.make_async_remote_copy(
            src_ref=outbuf.at[u],
            dst_ref=inbuf.at[u],
            send_sem=hop_send.at[u],
            recv_sem=arrive.at[u],
            device_id={"section": lax.rem(section + 1, sections)},
            device_id_type=MESH,
        )

    def arrival(slot):
        return pltpu.make_async_copy(inbuf.at[slot], inbuf.at[slot], arrive.at[slot])

    tubes_own = units * tubes_unit
    tubes_pair = 2 * tubes_unit
    batches = ((0, tubes_own - tubes_pair), (tubes_own - tubes_pair, tubes_pair))
    film_targets = [
        (target, step)
        for target in range(sections)
        for step in range(shards)
        if not (target == last and step == 0)
    ]

    def film_copy(batch, target, step):
        start, count = batches[batch]
        return pltpu.make_async_remote_copy(
            src_ref=pooled_out.at[target, pl.ds(start, count)],
            dst_ref=film_in.at[shard, pl.ds(start, count)],
            send_sem=film_send.at[batch, target, step],
            recv_sem=film_recv.at[batch, shard],
            device_id={"section": target, "dp": lax.rem(shard + step, shards)},
            device_id_type=MESH,
        )

    def film_arrival(batch, source):
        start, count = batches[batch]
        return pltpu.make_async_copy(
            film_in.at[source, pl.ds(start, count)],
            film_in.at[source, pl.ds(start, count)],
            film_recv.at[batch, source],
        )

    pooling_shape = (tubes_pair, 2 * unit_rows)
    pooling = jnp.where(
        iota(pooling_shape, 1) // PATCHES == iota(pooling_shape, 0), 1.0 / PATCHES, 0.0
    ).astype(BF16)

    def pool(p):
        rows = pl.ds(pl.multiple_of(p * tubes_pair, tubes_pair), tubes_pair)
        for target in range(sections):
            both = jnp.concatenate([outbuf[2 * p, target], outbuf[2 * p + 1, target]], axis=0)
            pooled = dot(pooling, both).astype(BF16)
            if target == last:
                film_in[shard, rows] = pooled
            else:
                pooled_out[target, rows] = pooled
            if target == last:
                pooled_out[target, rows] = pooled

    def exchange(stage, outgoing, incoming):
        copies = []
        for step in range(sections - 1, 0, -1):
            target = lax.rem(section + step, sections)
            copies.append(
                pltpu.make_async_remote_copy(
                    src_ref=outgoing(target),
                    dst_ref=incoming.at[section],
                    send_sem=ex_send.at[stage, step],
                    recv_sem=ex_recv.at[stage, section],
                    device_id={"section": target},
                    device_id_type=MESH,
                )
            )
        for copy in copies:
            copy.start()

        def arrivals():
            for step in range(1, sections):
                source = lax.rem(section + step, sections)
                pltpu.make_async_copy(
                    incoming.at[source], incoming.at[source], ex_recv.at[stage, source]
                ).wait()

        def sent():
            for copy in copies:
                copy.wait_send()

        return arrivals, sent

    head_arrivals, head_sent = exchange(3, lambda target: own_head, all_head)
    all_head[section] = own_head[...]

    for load in loads[:4]:
        load.wait()
    for load in loads[4:]:
        load.start()

    blocks = max(1, COLUMNS // channels)

    def run_unit(u):
        arrival(u).wait()
        stream = jnp.concatenate([inbuf[u, source] for source in range(sections)], axis=1)

        def emit(residual, gated):
            for first in range(0, sections, blocks):
                columns = slice(first * channels, (first + blocks) * channels)
                result = (residual[:, columns] + dot(gated, v_down[:, columns])).astype(BF16)
                for block in range(blocks):
                    outbuf[u, first + block] = result[:, block * channels : (block + 1) * channels]

        backbone_layer(stream.astype(F32), gains, v_qkv, v_out, v_up, emit)

        @pl.when(section < last)
        def _():
            hop(u).start()

        @pl.when((section == last) & (u % 2 == 1))
        def _():
            pool(u // 2)
            for batch, unit in ((0, units - 3), (1, units - 1)):

                @pl.when((u == unit) if STOP >= 1 else False)
                def _():
                    for target, step in film_targets:
                        film_copy(batch, target, step).start()

    each_unit(run_unit)

    def finish():
        head_arrivals()
        head_sent()

        @pl.when(section > 0)
        def _():
            each_unit(lambda u: patch_copy(u).wait_send())

        @pl.when(section < last)
        def _():
            each_unit(lambda u: hop(u).wait_send())

        @pl.when((section == last) if STOP >= 1 else False)
        def _():
            for batch in (0, 1):
                for target, step in film_targets:
                    film_copy(batch, target, step).wait_send()

    loads[4].wait()
    loads[5].wait()
    if STOP < 9:
        heads[...] = jnp.zeros(heads.shape, F32)
    if STOP == 0:
        return finish()

    for batch in (0, 1):

        @pl.when(section < last)
        def _():
            film_arrival(batch, shard).wait()

        for step in range(1, shards):
            film_arrival(batch, lax.rem(shard + step, shards)).wait()
    if STOP == 1:
        return finish()

    tubes = shards * tubes_own
    pooled = film_in[...].reshape(tubes, channels)
    clips = tubes // TUB_CLIP
    spread_shape = (clips, tubes)
    spread = jnp.where(iota(spread_shape, 1) // TUB_CLIP == iota(spread_shape, 0), 1.0, 0.0)
    slots = jnp.broadcast_to(clip_slot[...].astype(F32), (8, clips)).astype(BF16)
    position = TUB_CLIP * dot(slots, spread.astype(BF16))[0:1]
    position = position + (iota((1, tubes), 1) % TUB_CLIP).astype(F32)

    two_rows = two_out.shape[0]
    one_rows = 3 * two_rows
    row = iota((one_rows, 1), 0)
    level_index = 2 * (shard * two_rows + row % two_rows) + row // two_rows - 1
    taps = []
    for tap in range(3):
        wanted = (2 * level_index + tap - 1).astype(F32)
        selector = jnp.where(position == wanted, 1.0, 0.0).astype(BF16)
        taps.append(dot(selector, pooled).astype(BF16))

    def conv(parts, weight):
        total = dot(parts[0], weight[0])
        for tap in (1, 2):
            total = total + dot(parts[tap], weight[tap])
        return total.astype(BF16)

    def total(incoming):
        value = incoming[0].astype(F32)
        for source in range(1, sections):
            value = value + incoming[source].astype(F32)
        return value

    partial = conv(taps, v_one)
    for target in range(sections):
        one_out[target] = partial[:, target * channels : (target + 1) * channels]
    arrivals, one_sent = exchange(0, lambda target: one_out.at[target], one_in)
    one_in[section] = one_out[section]
    finish()
    arrivals()
    one = gelu(total(one_in)).astype(BF16)

    natural = 2 * two_rows
    order = (natural, one_rows)
    chosen = iota(order, 1) == (1 + iota(order, 0) % 2) * two_rows + iota(order, 0) // 2
    one_natural = dot(jnp.where(chosen, 1.0, 0.0).astype(BF16), one).astype(BF16)
    two_out[...] = conv([one[block * two_rows : (block + 1) * two_rows] for block in range(3)], v_two)
    two_arrivals, two_sent = exchange(1, lambda target: two_out, two_in)
    part_out[...] = dot_nt(own_head[...], one_natural)
    part_arrivals, part_sent = exchange(2, lambda target: part_out, part_in)
    two_in[section] = two_out[...]
    part_in[section] = part_out[...]
    one_sent()
    two_arrivals()
    two = gelu(total(two_in)).astype(BF16)
    every_head = jnp.concatenate([all_head[source] for source in range(sections)], axis=1)
    level_two = dot_nt(two, every_head)
    part_arrivals()
    heads[0 : own_head.shape[0], 0:natural] = total(part_in)
    heads[own_head.shape[0] :, 0 : own_head.shape[0]] = level_two
    two_sent()
    part_sent()


def split_heads(heads, head_one, head_two):
    outputs, natural = head_one.shape
    two_rows = head_two.shape[0]
    head_one[...] = heads[0:outputs, 0:natural]
    head_two[...] = heads[heads.shape[0] - two_rows :, 0:outputs]


def on_device(
    patches,
    clip_slot,
    w_qkv,
    w_out,
    w_up,
    w_down,
    norm_gains,
    level_one_weight,
    level_two_weight,
    head_weight,
):
    sections = lax.axis_size("section")
    shards = lax.axis_size("dp")
    rows, channels = patches.shape
    width = channels * sections
    unit_rows = UNIT_ROWS
    units = rows // unit_rows
    tubes_unit = unit_rows // PATCHES
    outputs = head_weight.shape[1]
    one_rows = rows // PATCHES // 2
    two_rows = one_rows // 2
    vmem = pl.BlockSpec(memory_space=pltpu.VMEM)
    anywhere = pl.BlockSpec(memory_space=pl.ANY)
    dma = pltpu.SemaphoreType.DMA
    head_rows = -(-outputs // 16) * 16
    heads = pl.pallas_call(
        functools.partial(kernel, sections, shards),
        out_shape=jax.ShapeDtypeStruct((head_rows + two_rows, 128), F32),
        in_specs=[anywhere, vmem] + [anywhere] * 4 + [vmem] + [anywhere] * 2 + [vmem],
        out_specs=vmem,
        scratch_shapes=[
            pltpu.VMEM(w_qkv.shape[1:], BF16),
            pltpu.VMEM(w_out.shape[1:], BF16),
            pltpu.VMEM(w_up.shape[1:], BF16),
            pltpu.VMEM(w_down.shape[1:], BF16),
            pltpu.VMEM(level_one_weight.shape, BF16),
            pltpu.VMEM(level_two_weight.shape, BF16),
            pltpu.VMEM(patches.shape, BF16),
            pltpu.VMEM((units, sections, unit_rows, channels), BF16),
            pltpu.VMEM((units, sections, unit_rows, channels), BF16),
            pltpu.VMEM((sections, units * tubes_unit, channels), BF16),
            pltpu.VMEM((shards, units * tubes_unit, channels), BF16),
            pltpu.VMEM((sections, 3 * two_rows, channels), BF16),
            pltpu.VMEM((sections, 3 * two_rows, channels), BF16),
            pltpu.VMEM((two_rows, width), BF16),
            pltpu.VMEM((sections, two_rows, width), BF16),
            pltpu.VMEM((head_rows, 2 * two_rows), F32),
            pltpu.VMEM((sections, head_rows, 2 * two_rows), F32),
            pltpu.VMEM((head_rows, channels), BF16),
            pltpu.VMEM((sections, head_rows, channels), BF16),
            dma((7,)),
            dma((units,)),
            dma((units,)),
            dma((units,)),
            dma((2, sections, shards)),
            dma((2, shards)),
            dma((4, sections)),
            dma((4, sections)),
        ],
        compiler_params=pltpu.CompilerParams(
            collective_id=0, has_side_effects=True, vmem_limit_bytes=60 * 1024 * 1024
        ),
    )(
        patches,
        clip_slot.reshape(1, -1),
        w_qkv,
        w_out,
        w_up,
        w_down,
        norm_gains,
        level_one_weight,
        level_two_weight,
        head_weight.T,
    )
    head_one, head_two = pl.pallas_call(
        split_heads,
        out_shape=(
            jax.ShapeDtypeStruct((outputs, one_rows), F32),
            jax.ShapeDtypeStruct((two_rows, outputs), F32),
        ),
        in_specs=[vmem],
        out_specs=(vmem, vmem),
    )(heads)
    return head_one.T, head_two


def solution(mesh):
    return jax.shard_map(
        on_device,
        mesh=mesh,
        in_specs=(
            P(("groups", "dp"), "section"),
            P("groups"),
            P("section", None, None),
            P("section", None, None),
            P("section", None, None),
            P("section", None, None),
            P("section", None, None),
            P(None, "section", None),
            P(None, "section", None),
            P("section", None),
        ),
        out_specs=(P(("groups", "dp"), None), P(("groups", "dp"), None)),
        check_vma=False,
    )
```

```python
import functools

import jax
import jax.numpy as jnp
from jax import lax
from jax.experimental import pallas as pl
from jax.experimental.pallas import tpu as pltpu
from jax.sharding import PartitionSpec as P

HEADS = 8
HEAD = 64
PATCHES = 16
TUB_CLIP = 2
EPSILON = 1e-05
UNIT_ROWS = 128
ROW_BLOCK = 128
CHUNK = 512
COLUMNS = 256
STOP = 9
MESH = pl.DeviceIdType.MESH
F32 = jnp.float32
BF16 = jnp.bfloat16


def dot(a, b):
    return jnp.dot(a, b, preferred_element_type=F32)


def dot_nt(a, b):
    return lax.dot_general(a, b, (((1,), (1,)), ((), ())), preferred_element_type=F32)


def gelu(values):
    return jax.nn.gelu(values, approximate=True)


def gelu_rounded(values):
    x = values.astype(BF16)
    inner = x * (x * x * 0.035677408136300125 + 0.7978845608028654)
    return x * (jnp.tanh(inner) * 0.5 + 0.5)


def iota(shape, dim):
    return lax.broadcasted_iota(jnp.int32, shape, dim)


def centre(values, scaling):
    average = jnp.mean(values, axis=-1, keepdims=True)
    square = jnp.mean(values * values, axis=-1, keepdims=True)
    spread = jnp.maximum(square - average * average, 0.0) + EPSILON
    return ((values - average) * scaling).astype(BF16), spread


def backbone_layer(stream, gains, v_qkv, v_out, v_up, averaging, own, clip_mask, emit):
    inner = v_out.shape[0]
    hidden = v_up.shape[1]
    pair = 2 * HEAD
    group = averaging.shape[0]
    normed, spread = centre(stream, gains[0, 0:1])
    raw = []
    for start in range(0, inner, group):
        raw.append(
            (
                dot(normed, v_qkv[:, start : start + group]),
                dot(normed, v_qkv[:, inner + start : inner + start + group]),
            )
        )
    floor = EPSILON * spread

    def head_scale(part):
        return part * lax.rsqrt(dot((part * part).astype(BF16), averaging[...]) + floor)

    scaled = [
        ((head_scale(raw_q) * HEAD**-0.5).astype(BF16), head_scale(raw_k).astype(BF16))
        for raw_q, raw_k in raw
    ]
    scale = lax.rsqrt(spread)
    values = [
        (dot(normed, v_qkv[:, 2 * inner + start : 2 * inner + start + group]) * scale).astype(BF16)
        for start in range(0, inner, group)
    ]
    scores = []
    stacked = []
    for (query, key), value in zip(scaled, values):
        for lane in range(0, group, pair):
            k = key[:, lane : lane + pair]
            v = value[:, lane : lane + pair]
            k2 = jnp.concatenate([k, k], axis=0) * own[...]
            v2 = jnp.concatenate([v, v], axis=0) * own[...]
            scores.append(dot_nt(query[:, lane : lane + pair], k2))
            stacked.append(jnp.concatenate([v2, own[...]], axis=1))
    weights = [jnp.exp(score).astype(BF16) * clip_mask[...] for score in scores]
    mixed = []
    for weight, stack in zip(weights, stacked):
        both = dot(weight, stack)
        mixed.append((both[:, :pair] / both[:, pair:]).astype(BF16))
    residual = stream + dot(jnp.concatenate(mixed, axis=1), v_out[...])
    normed_b, spread_b = centre(residual, gains[0, 1:2])
    scale_b = lax.rsqrt(spread_b)
    parts = [
        gelu_rounded(dot(normed_b, v_up[:, start : start + CHUNK]) * scale_b)
        for start in range(0, hidden, CHUNK)
    ]
    emit(residual, jnp.concatenate(parts, axis=1))


def kernel(
    sections,
    shards,
    patches,
    clip_slot,
    w_qkv,
    w_out,
    w_up,
    w_down,
    gains,
    one_weight,
    two_weight,
    head_weight,
    heads,
    v_qkv,
    v_out,
    v_up,
    v_down,
    v_one,
    v_two,
    patch_buf,
    inbuf,
    outbuf,
    pooled_out,
    film_in,
    one_out,
    one_in,
    two_out,
    two_in,
    part_out,
    part_in,
    own_head,
    all_head,
    averaging,
    own,
    clip_mask,
    selector,
    weight_sem,
    gather_send,
    arrive,
    hop_send,
    film_send,
    film_recv,
    ex_send,
    ex_recv,
):
    section = lax.axis_index("section")
    shard = lax.axis_index("dp")
    last = sections - 1
    units, _, unit_rows, channels = outbuf.shape
    width = sections * channels
    tubes_unit = unit_rows // PATCHES
    outputs = head_weight.shape[0]
    loads = [
        pltpu.make_async_copy(source, target, weight_sem.at[index])
        for index, (source, target) in enumerate(
            (
                (w_qkv.at[0], v_qkv),
                (w_out.at[0], v_out),
                (w_up.at[0], v_up),
                (w_down.at[0], v_down),
                (one_weight, v_one),
                (two_weight, v_two),
            )
        )
    ]
    def each_unit(body):
        def step(u, carry):
            body(u)
            return carry

        lax.fori_loop(0, units, step, 0)

    def patch_rows(u):
        return pl.ds(pl.multiple_of(u * unit_rows, unit_rows), unit_rows)

    patch_load = pltpu.make_async_copy(patches, patch_buf, weight_sem.at[6])

    @pl.when(section > 0)
    def _():
        patch_load.start()

    @pl.when(section == 0)
    def _():
        each_unit(
            lambda u: pltpu.make_async_copy(
                patches.at[patch_rows(u)], inbuf.at[u, 0], arrive.at[u]
            ).start()
        )

    for load in loads[:4]:
        load.start()
    own_head[...] = jnp.zeros(own_head.shape, BF16)
    own_head[0:outputs] = head_weight[...]

    same = iota(averaging.shape, 0) // HEAD == iota(averaging.shape, 1) // HEAD
    averaging[...] = jnp.where(same, 1.0 / HEAD, 0.0).astype(BF16)
    mine = (iota(own.shape, 0) < unit_rows) == (iota(own.shape, 1) < HEAD)
    own[...] = jnp.where(mine, 1.0, 0.0).astype(BF16)
    clip = PATCHES * TUB_CLIP
    same_clip = iota(clip_mask.shape, 0) // clip == iota(clip_mask.shape, 1) % unit_rows // clip
    clip_mask[...] = jnp.where(same_clip, 1.0, 0.0).astype(BF16)

    barrier = pltpu.get_barrier_semaphore()
    for ds in range(sections):
        for dd in range(shards):
            if ds or dd:
                pl.semaphore_signal(
                    barrier,
                    inc=1,
                    device_id={
                        "section": lax.rem(section + ds, sections),
                        "dp": lax.rem(shard + dd, shards),
                    },
                    device_id_type=MESH,
                )
    pl.semaphore_wait(barrier, sections * shards - 1)

    def patch_copy(u):
        return pltpu.make_async_remote_copy(
            src_ref=patch_buf.at[patch_rows(u)],
            dst_ref=inbuf.at[u, section],
            send_sem=gather_send.at[u],
            recv_sem=arrive.at[u],
            device_id={"section": 0},
            device_id_type=MESH,
        )

    @pl.when(section > 0)
    def _():
        patch_load.wait()
        each_unit(lambda u: patch_copy(u).start())

    def hop(u):
        return pltpu.make_async_remote_copy(
            src_ref=outbuf.at[u],
            dst_ref=inbuf.at[u],
            send_sem=hop_send.at[u],
            recv_sem=arrive.at[u],
            device_id={"section": lax.rem(section + 1, sections)},
            device_id_type=MESH,
        )

    def arrival(slot):
        return pltpu.make_async_copy(inbuf.at[slot], inbuf.at[slot], arrive.at[slot])

    tubes_own = units * tubes_unit
    tubes_pair = 2 * tubes_unit
    batches = ((0, tubes_own - tubes_pair), (tubes_own - tubes_pair, tubes_pair))
    film_targets = [
        (target, step)
        for target in range(sections)
        for step in range(shards)
        if not (target == last and step == 0)
    ]

    def film_copy(batch, target, step):
        start, count = batches[batch]
        return pltpu.make_async_remote_copy(
            src_ref=pooled_out.at[target, pl.ds(start, count)],
            dst_ref=film_in.at[shard, pl.ds(start, count)],
            send_sem=film_send.at[batch, target, step],
            recv_sem=film_recv.at[batch, shard],
            device_id={"section": target, "dp": lax.rem(shard + step, shards)},
            device_id_type=MESH,
        )

    def film_arrival(batch, source):
        start, count = batches[batch]
        return pltpu.make_async_copy(
            film_in.at[source, pl.ds(start, count)],
            film_in.at[source, pl.ds(start, count)],
            film_recv.at[batch, source],
        )

    pooling_shape = (tubes_pair, 2 * unit_rows)
    pooling = jnp.where(
        iota(pooling_shape, 1) // PATCHES == iota(pooling_shape, 0), 1.0 / PATCHES, 0.0
    ).astype(BF16)

    def pool(p):
        rows = pl.ds(pl.multiple_of(p * tubes_pair, tubes_pair), tubes_pair)
        for target in range(sections):
            both = jnp.concatenate([outbuf[2 * p, target], outbuf[2 * p + 1, target]], axis=0)
            pooled = dot(pooling, both).astype(BF16)
            if target == last:
                film_in[shard, rows] = pooled
            else:
                pooled_out[target, rows] = pooled
            if target == last:
                pooled_out[target, rows] = pooled

    def exchange(stage, outgoing, incoming):
        copies = []
        for step in range(sections - 1, 0, -1):
            target = lax.rem(section + step, sections)
            copies.append(
                pltpu.make_async_remote_copy(
                    src_ref=outgoing(target),
                    dst_ref=incoming.at[section],
                    send_sem=ex_send.at[stage, step],
                    recv_sem=ex_recv.at[stage, section],
                    device_id={"section": target},
                    device_id_type=MESH,
                )
            )
        for copy in copies:
            copy.start()

        def arrivals():
            for step in range(1, sections):
                source = lax.rem(section + step, sections)
                pltpu.make_async_copy(
                    incoming.at[source], incoming.at[source], ex_recv.at[stage, source]
                ).wait()

        def sent():
            for copy in copies:
                copy.wait_send()

        return arrivals, sent

    head_arrivals, head_sent = exchange(3, lambda target: own_head, all_head)
    all_head[section] = own_head[...]

    tubes = selector.shape[1]
    clips = tubes // TUB_CLIP
    spread_shape = (clips, tubes)
    spread = jnp.where(iota(spread_shape, 1) // TUB_CLIP == iota(spread_shape, 0), 1.0, 0.0)
    slots = jnp.broadcast_to(clip_slot[...].astype(F32), (8, clips)).astype(BF16)
    position = TUB_CLIP * dot(slots, spread.astype(BF16))[0:1]
    position = position + (iota((1, tubes), 1) % TUB_CLIP).astype(F32)
    two_rows = two_out.shape[0]
    one_rows = 3 * two_rows
    row = iota((one_rows, 1), 0)
    level_index = 2 * (shard * two_rows + row % two_rows) + row // two_rows - 1
    for tap in range(3):
        wanted = (2 * level_index + tap - 1).astype(F32)
        chosen = jnp.where(position == wanted, 1.0, 0.0).astype(BF16)
        selector[tap * one_rows : (tap + 1) * one_rows] = chosen

    for load in loads[:4]:
        load.wait()
    for load in loads[4:]:
        load.start()

    blocks = max(1, COLUMNS // channels)

    def run_unit(u):
        arrival(u).wait()
        stream = jnp.concatenate([inbuf[u, source] for source in range(sections)], axis=1)

        def emit(residual, gated):
            for first in range(0, sections, blocks):
                columns = slice(first * channels, (first + blocks) * channels)
                result = (residual[:, columns] + dot(gated, v_down[:, columns])).astype(BF16)
                for block in range(blocks):
                    outbuf[u, first + block] = result[:, block * channels : (block + 1) * channels]

        backbone_layer(
            stream.astype(F32), gains, v_qkv, v_out, v_up, averaging, own, clip_mask, emit
        )

        @pl.when(section < last)
        def _():
            hop(u).start()

        @pl.when((section == last) & (u % 2 == 1))
        def _():
            pool(u // 2)
            for batch, unit in ((0, units - 3), (1, units - 1)):

                @pl.when((u == unit) if STOP >= 1 else False)
                def _():
                    for target, step in film_targets:
                        film_copy(batch, target, step).start()

    each_unit(run_unit)

    def finish():
        head_arrivals()
        head_sent()

        @pl.when(section > 0)
        def _():
            each_unit(lambda u: patch_copy(u).wait_send())

        @pl.when(section < last)
        def _():
            each_unit(lambda u: hop(u).wait_send())

        @pl.when((section == last) if STOP >= 1 else False)
        def _():
            for batch in (0, 1):
                for target, step in film_targets:
                    film_copy(batch, target, step).wait_send()

    loads[4].wait()
    loads[5].wait()
    if STOP < 9:
        heads[...] = jnp.zeros(heads.shape, F32)
    if STOP == 0:
        return finish()

    for batch in (0, 1):

        @pl.when(section < last)
        def _():
            film_arrival(batch, shard).wait()

        for step in range(1, shards):
            film_arrival(batch, lax.rem(shard + step, shards)).wait()
    if STOP == 1:
        return finish()

    pooled = film_in[...].reshape(tubes, channels)
    picked = dot(selector[...], pooled).astype(BF16)
    taps = [picked[tap * one_rows : (tap + 1) * one_rows] for tap in range(3)]

    def conv(parts, weight):
        total = dot(parts[0], weight[0])
        for tap in (1, 2):
            total = total + dot(parts[tap], weight[tap])
        return total.astype(BF16)

    def total(incoming):
        value = incoming[0].astype(F32)
        for source in range(1, sections):
            value = value + incoming[source].astype(F32)
        return value

    partial = conv(taps, v_one)
    for target in range(sections):
        one_out[target] = partial[:, target * channels : (target + 1) * channels]
    arrivals, one_sent = exchange(0, lambda target: one_out.at[target], one_in)
    one_in[section] = one_out[section]
    finish()
    arrivals()
    one = gelu(total(one_in)).astype(BF16)

    natural = 2 * two_rows
    order = (natural, one_rows)
    chosen = iota(order, 1) == (1 + iota(order, 0) % 2) * two_rows + iota(order, 0) // 2
    one_natural = dot(jnp.where(chosen, 1.0, 0.0).astype(BF16), one).astype(BF16)
    two_out[...] = conv([one[block * two_rows : (block + 1) * two_rows] for block in range(3)], v_two)
    two_arrivals, two_sent = exchange(1, lambda target: two_out, two_in)
    part_out[...] = dot_nt(own_head[...], one_natural)
    part_arrivals, part_sent = exchange(2, lambda target: part_out, part_in)
    two_in[section] = two_out[...]
    part_in[section] = part_out[...]
    one_sent()
    two_arrivals()
    two = gelu(total(two_in)).astype(BF16)
    every_head = jnp.concatenate([all_head[source] for source in range(sections)], axis=1)
    level_two = dot_nt(two, every_head)
    part_arrivals()
    heads[0 : own_head.shape[0], 0:natural] = total(part_in)
    heads[own_head.shape[0] :, 0 : own_head.shape[0]] = level_two
    two_sent()
    part_sent()


def split_heads(heads, head_one, head_two):
    outputs, natural = head_one.shape
    two_rows = head_two.shape[0]
    head_one[...] = heads[0:outputs, 0:natural]
    head_two[...] = heads[heads.shape[0] - two_rows :, 0:outputs]


def on_device(
    patches,
    clip_slot,
    w_qkv,
    w_out,
    w_up,
    w_down,
    norm_gains,
    level_one_weight,
    level_two_weight,
    head_weight,
):
    sections = lax.axis_size("section")
    shards = lax.axis_size("dp")
    rows, channels = patches.shape
    width = channels * sections
    unit_rows = UNIT_ROWS
    units = rows // unit_rows
    tubes_unit = unit_rows // PATCHES
    outputs = head_weight.shape[1]
    one_rows = rows // PATCHES // 2
    two_rows = one_rows // 2
    vmem = pl.BlockSpec(memory_space=pltpu.VMEM)
    anywhere = pl.BlockSpec(memory_space=pl.ANY)
    dma = pltpu.SemaphoreType.DMA
    group = min(256, w_out.shape[1])
    head_rows = -(-outputs // 16) * 16
    heads = pl.pallas_call(
        functools.partial(kernel, sections, shards),
        out_shape=jax.ShapeDtypeStruct((head_rows + two_rows, 128), F32),
        in_specs=[anywhere, vmem] + [anywhere] * 4 + [vmem] + [anywhere] * 2 + [vmem],
        out_specs=vmem,
        scratch_shapes=[
            pltpu.VMEM(w_qkv.shape[1:], BF16),
            pltpu.VMEM(w_out.shape[1:], BF16),
            pltpu.VMEM(w_up.shape[1:], BF16),
            pltpu.VMEM(w_down.shape[1:], BF16),
            pltpu.VMEM(level_one_weight.shape, BF16),
            pltpu.VMEM(level_two_weight.shape, BF16),
            pltpu.VMEM(patches.shape, BF16),
            pltpu.VMEM((units, sections, unit_rows, channels), BF16),
            pltpu.VMEM((units, sections, unit_rows, channels), BF16),
            pltpu.VMEM((sections, units * tubes_unit, channels), BF16),
            pltpu.VMEM((shards, units * tubes_unit, channels), BF16),
            pltpu.VMEM((sections, 3 * two_rows, channels), BF16),
            pltpu.VMEM((sections, 3 * two_rows, channels), BF16),
            pltpu.VMEM((two_rows, width), BF16),
            pltpu.VMEM((sections, two_rows, width), BF16),
            pltpu.VMEM((head_rows, 2 * two_rows), F32),
            pltpu.VMEM((sections, head_rows, 2 * two_rows), F32),
            pltpu.VMEM((head_rows, channels), BF16),
            pltpu.VMEM((sections, head_rows, channels), BF16),
            pltpu.VMEM((group, group), BF16),
            pltpu.VMEM((2 * unit_rows, 2 * HEAD), BF16),
            pltpu.VMEM((unit_rows, 2 * unit_rows), BF16),
            pltpu.VMEM((9 * two_rows, shards * units * tubes_unit), BF16),
            dma((7,)),
            dma((units,)),
            dma((units,)),
            dma((units,)),
            dma((2, sections, shards)),
            dma((2, shards)),
            dma((4, sections)),
            dma((4, sections)),
        ],
        compiler_params=pltpu.CompilerParams(
            collective_id=0, has_side_effects=True, vmem_limit_bytes=60 * 1024 * 1024
        ),
    )(
        patches,
        clip_slot.reshape(1, -1),
        w_qkv,
        w_out,
        w_up,
        w_down,
        norm_gains,
        level_one_weight,
        level_two_weight,
        head_weight.T,
    )
    head_one, head_two = pl.pallas_call(
        split_heads,
        out_shape=(
            jax.ShapeDtypeStruct((outputs, one_rows), F32),
            jax.ShapeDtypeStruct((two_rows, outputs), F32),
        ),
        in_specs=[vmem],
        out_specs=(vmem, vmem),
    )(heads)
    return head_one.T, head_two


def solution(mesh):
    return jax.shard_map(
        on_device,
        mesh=mesh,
        in_specs=(
            P(("groups", "dp"), "section"),
            P("groups"),
            P("section", None, None),
            P("section", None, None),
            P("section", None, None),
            P("section", None, None),
            P("section", None, None),
            P(None, "section", None),
            P(None, "section", None),
            P("section", None),
        ),
        out_specs=(P(("groups", "dp"), None), P(("groups", "dp"), None)),
        check_vma=False,
    )
```

```python
import functools

import jax
import jax.numpy as jnp
from jax import lax
from jax.experimental import pallas as pl
from jax.experimental.pallas import tpu as pltpu
from jax.sharding import PartitionSpec as P

HEADS = 8
HEAD = 64
PATCHES = 16
TUB_CLIP = 2
EPSILON = 1e-05
UNIT_ROWS = 128
ROW_BLOCK = 128
CHUNK = 512
COLUMNS = 256
STOP = 9
MESH = pl.DeviceIdType.MESH
F32 = jnp.float32
BF16 = jnp.bfloat16


def dot(a, b):
    return jnp.dot(a, b, preferred_element_type=F32)


def dot_nt(a, b):
    return lax.dot_general(a, b, (((1,), (1,)), ((), ())), preferred_element_type=F32)


def gelu(values):
    return jax.nn.gelu(values, approximate=True)


def gelu_rounded(values):
    x = values.astype(BF16)
    inner = x * (x * x * 0.035677408136300125 + 0.7978845608028654)
    return x * (jnp.tanh(inner) * 0.5 + 0.5)


def iota(shape, dim):
    return lax.broadcasted_iota(jnp.int32, shape, dim)


def centre(values, scaling):
    average = jnp.mean(values, axis=-1, keepdims=True)
    square = jnp.mean(values * values, axis=-1, keepdims=True)
    spread = jnp.maximum(square - average * average, 0.0) + EPSILON
    return ((values - average) * scaling).astype(BF16), spread


def backbone_layer(stream, gains, v_qkv, v_out, v_up, averaging, own, clip_mask, emit):
    inner = v_out.shape[0]
    hidden = v_up.shape[1]
    pair = 2 * HEAD
    group = averaging.shape[0]
    normed, spread = centre(stream, gains[0, 0:1])
    raw = []
    for start in range(0, inner, group):
        raw.append(
            (
                dot(normed, v_qkv[:, start : start + group]),
                dot(normed, v_qkv[:, inner + start : inner + start + group]),
            )
        )
    floor = EPSILON * spread

    def head_scale(part):
        return part * lax.rsqrt(dot((part * part).astype(BF16), averaging[...]) + floor)

    scaled = [
        ((head_scale(raw_q) * HEAD**-0.5).astype(BF16), head_scale(raw_k).astype(BF16))
        for raw_q, raw_k in raw
    ]
    scale = lax.rsqrt(spread)
    values = [
        (dot(normed, v_qkv[:, 2 * inner + start : 2 * inner + start + group]) * scale).astype(BF16)
        for start in range(0, inner, group)
    ]
    scores = []
    stacked = []
    for (query, key), value in zip(scaled, values):
        for lane in range(0, group, pair):
            k = key[:, lane : lane + pair]
            v = value[:, lane : lane + pair]
            k2 = jnp.concatenate([k, k], axis=0) * own[...]
            v2 = jnp.concatenate([v, v], axis=0) * own[...]
            scores.append(dot_nt(query[:, lane : lane + pair], k2))
            stacked.append(jnp.concatenate([v2, own[...]], axis=1))
    weights = [jnp.exp(score).astype(BF16) * clip_mask[...] for score in scores]
    mixed = []
    for weight, stack in zip(weights, stacked):
        both = dot(weight, stack)
        mixed.append((both[:, :pair] / both[:, pair:]).astype(BF16))
    residual = stream + dot(jnp.concatenate(mixed, axis=1), v_out[...])
    normed_b, spread_b = centre(residual, gains[0, 1:2])
    scale_b = lax.rsqrt(spread_b)
    parts = [
        gelu_rounded(dot(normed_b, v_up[:, start : start + CHUNK]) * scale_b)
        for start in range(0, hidden, CHUNK)
    ]
    emit(residual, jnp.concatenate(parts, axis=1))


def kernel(
    sections,
    shards,
    patches,
    slot_in,
    w_qkv,
    w_out,
    w_up,
    w_down,
    gains_in,
    one_weight,
    two_weight,
    head_in,
    heads,
    v_qkv,
    v_out,
    v_up,
    v_down,
    v_one,
    v_two,
    patch_buf,
    inbuf,
    outbuf,
    pooled_out,
    film_in,
    one_out,
    one_in,
    two_out,
    two_in,
    part_out,
    part_in,
    own_head,
    all_head,
    averaging,
    own,
    clip_mask,
    selector,
    clip_slot,
    gains,
    head_weight,
    weight_sem,
    gather_send,
    arrive,
    hop_send,
    film_send,
    film_recv,
    ex_send,
    ex_recv,
):
    section = lax.axis_index("section")
    shard = lax.axis_index("dp")
    last = sections - 1
    units, _, unit_rows, channels = outbuf.shape
    width = sections * channels
    tubes_unit = unit_rows // PATCHES
    outputs = head_weight.shape[0]
    loads = [
        pltpu.make_async_copy(source, target, weight_sem.at[index])
        for index, (source, target) in enumerate(
            (
                (w_qkv.at[0], v_qkv),
                (w_out.at[0], v_out),
                (w_up.at[0], v_up),
                (w_down.at[0], v_down),
                (one_weight, v_one),
                (two_weight, v_two),
            )
        )
    ]
    def each_unit(body):
        def step(u, carry):
            body(u)
            return carry

        lax.fori_loop(0, units, step, 0)

    def patch_rows(u):
        return pl.ds(pl.multiple_of(u * unit_rows, unit_rows), unit_rows)

    patch_load = pltpu.make_async_copy(patches, patch_buf, weight_sem.at[6])

    @pl.when(section > 0)
    def _():
        patch_load.start()

    @pl.when(section == 0)
    def _():
        each_unit(
            lambda u: pltpu.make_async_copy(
                patches.at[patch_rows(u)], inbuf.at[u, 0], arrive.at[u]
            ).start()
        )

    small = [
        pltpu.make_async_copy(source, target, weight_sem.at[7 + index])
        for index, (source, target) in enumerate(
            ((slot_in, clip_slot), (gains_in, gains), (head_in, head_weight))
        )
    ]
    for load in small + loads[:4]:
        load.start()

    same = iota(averaging.shape, 0) // HEAD == iota(averaging.shape, 1) // HEAD
    averaging[...] = jnp.where(same, 1.0 / HEAD, 0.0).astype(BF16)
    mine = (iota(own.shape, 0) < unit_rows) == (iota(own.shape, 1) < HEAD)
    own[...] = jnp.where(mine, 1.0, 0.0).astype(BF16)
    clip = PATCHES * TUB_CLIP
    same_clip = iota(clip_mask.shape, 0) // clip == iota(clip_mask.shape, 1) % unit_rows // clip
    clip_mask[...] = jnp.where(same_clip, 1.0, 0.0).astype(BF16)

    barrier = pltpu.get_barrier_semaphore()
    for ds in range(sections):
        for dd in range(shards):
            if ds or dd:
                pl.semaphore_signal(
                    barrier,
                    inc=1,
                    device_id={
                        "section": lax.rem(section + ds, sections),
                        "dp": lax.rem(shard + dd, shards),
                    },
                    device_id_type=MESH,
                )
    pl.semaphore_wait(barrier, sections * shards - 1)

    def patch_copy(u):
        return pltpu.make_async_remote_copy(
            src_ref=patch_buf.at[patch_rows(u)],
            dst_ref=inbuf.at[u, section],
            send_sem=gather_send.at[u],
            recv_sem=arrive.at[u],
            device_id={"section": 0},
            device_id_type=MESH,
        )

    @pl.when(section > 0)
    def _():
        patch_load.wait()
        each_unit(lambda u: patch_copy(u).start())

    def hop(u):
        return pltpu.make_async_remote_copy(
            src_ref=outbuf.at[u],
            dst_ref=inbuf.at[u],
            send_sem=hop_send.at[u],
            recv_sem=arrive.at[u],
            device_id={"section": lax.rem(section + 1, sections)},
            device_id_type=MESH,
        )

    def arrival(slot):
        return pltpu.make_async_copy(inbuf.at[slot], inbuf.at[slot], arrive.at[slot])

    tubes_own = units * tubes_unit
    tubes_pair = 2 * tubes_unit
    batches = ((0, tubes_own - tubes_pair), (tubes_own - tubes_pair, tubes_pair))
    film_targets = [
        (target, step)
        for target in range(sections)
        for step in range(shards)
        if not (target == last and step == 0)
    ]

    def film_copy(batch, target, step):
        start, count = batches[batch]
        return pltpu.make_async_remote_copy(
            src_ref=pooled_out.at[target, pl.ds(start, count)],
            dst_ref=film_in.at[shard, pl.ds(start, count)],
            send_sem=film_send.at[batch, target, step],
            recv_sem=film_recv.at[batch, shard],
            device_id={"section": target, "dp": lax.rem(shard + step, shards)},
            device_id_type=MESH,
        )

    def film_arrival(batch, source):
        start, count = batches[batch]
        return pltpu.make_async_copy(
            film_in.at[source, pl.ds(start, count)],
            film_in.at[source, pl.ds(start, count)],
            film_recv.at[batch, source],
        )

    pooling_shape = (tubes_pair, 2 * unit_rows)
    pooling = jnp.where(
        iota(pooling_shape, 1) // PATCHES == iota(pooling_shape, 0), 1.0 / PATCHES, 0.0
    ).astype(BF16)

    def pool(p):
        rows = pl.ds(pl.multiple_of(p * tubes_pair, tubes_pair), tubes_pair)
        for target in range(sections):
            both = jnp.concatenate([outbuf[2 * p, target], outbuf[2 * p + 1, target]], axis=0)
            pooled = dot(pooling, both).astype(BF16)
            if target == last:
                film_in[shard, rows] = pooled
            else:
                pooled_out[target, rows] = pooled
            if target == last:
                pooled_out[target, rows] = pooled

    def exchange(stage, outgoing, incoming, fill=None):
        copies = []
        for step in range(sections - 1, 0, -1):
            if fill is not None:
                fill(step)
            target = lax.rem(section + step, sections)
            copies.append(
                pltpu.make_async_remote_copy(
                    src_ref=outgoing(target),
                    dst_ref=incoming.at[section],
                    send_sem=ex_send.at[stage, step],
                    recv_sem=ex_recv.at[stage, section],
                    device_id={"section": target},
                    device_id_type=MESH,
                )
            )
            copies[-1].start()

        def arrivals():
            for step in range(1, sections):
                source = lax.rem(section + step, sections)
                pltpu.make_async_copy(
                    incoming.at[source], incoming.at[source], ex_recv.at[stage, source]
                ).wait()

        def sent():
            for copy in copies:
                copy.wait_send()

        return arrivals, sent

    for load in small:
        load.wait()
    own_head[...] = jnp.zeros(own_head.shape, BF16)
    own_head[0:outputs] = head_weight[...]
    head_arrivals, head_sent = exchange(3, lambda target: own_head, all_head)
    all_head[section] = own_head[...]

    tubes = selector.shape[1]
    clips = tubes // TUB_CLIP
    spread_shape = (clips, tubes)
    spread = jnp.where(iota(spread_shape, 1) // TUB_CLIP == iota(spread_shape, 0), 1.0, 0.0)
    slots = jnp.broadcast_to(clip_slot[...].astype(F32), (8, clips)).astype(BF16)
    position = TUB_CLIP * dot(slots, spread.astype(BF16))[0:1]
    position = position + (iota((1, tubes), 1) % TUB_CLIP).astype(F32)
    two_rows = two_out.shape[0]
    one_rows = 3 * two_rows
    row = iota((one_rows, 1), 0)
    level_index = 2 * (shard * two_rows + row % two_rows) + row // two_rows - 1
    for tap in range(3):
        wanted = (2 * level_index + tap - 1).astype(F32)
        chosen = jnp.where(position == wanted, 1.0, 0.0).astype(BF16)
        selector[tap * one_rows : (tap + 1) * one_rows] = chosen

    for load in loads[:4]:
        load.wait()
    for load in loads[4:]:
        load.start()

    blocks = max(1, COLUMNS // channels)

    def run_unit(u):
        arrival(u).wait()
        stream = jnp.concatenate([inbuf[u, source] for source in range(sections)], axis=1)

        def emit(residual, gated):
            for first in range(0, sections, blocks):
                columns = slice(first * channels, (first + blocks) * channels)
                result = (residual[:, columns] + dot(gated, v_down[:, columns])).astype(BF16)
                for block in range(blocks):
                    outbuf[u, first + block] = result[:, block * channels : (block + 1) * channels]

        backbone_layer(
            stream.astype(F32), gains, v_qkv, v_out, v_up, averaging, own, clip_mask, emit
        )

        @pl.when(section < last)
        def _():
            hop(u).start()

        @pl.when((section == last) & (u % 2 == 1))
        def _():
            pool(u // 2)
            for batch, unit in ((0, units - 3), (1, units - 1)):

                @pl.when((u == unit) if STOP >= 1 else False)
                def _():
                    for target, step in film_targets:
                        film_copy(batch, target, step).start()

    each_unit(run_unit)

    def film_sent(batch):
        @pl.when((section == last) if STOP >= 1 else False)
        def _():
            for target, step in film_targets:
                film_copy(batch, target, step).wait_send()

    def finish():
        head_arrivals()
        head_sent()

        @pl.when(section > 0)
        def _():
            each_unit(lambda u: patch_copy(u).wait_send())

        @pl.when(section < last)
        def _():
            each_unit(lambda u: hop(u).wait_send())

        film_sent(0)

    loads[4].wait()
    loads[5].wait()
    if STOP < 9:
        heads[...] = jnp.zeros(heads.shape, F32)
    finish()
    if STOP == 0:
        return

    for batch in (0, 1):

        @pl.when(section < last)
        def _():
            film_arrival(batch, shard).wait()

        for step in range(1, shards):
            film_arrival(batch, lax.rem(shard + step, shards)).wait()
    if STOP == 1:
        return film_sent(1)

    pooled = film_in[...].reshape(tubes, channels)
    picked = dot(selector[...], pooled).astype(BF16)
    taps = [picked[tap * one_rows : (tap + 1) * one_rows] for tap in range(3)]

    def conv(parts, weight, columns=slice(None)):
        total = dot(parts[0], weight[0, :, columns])
        for tap in (1, 2):
            total = total + dot(parts[tap], weight[tap, :, columns])
        return total.astype(BF16)

    def total(incoming):
        value = incoming[0].astype(F32)
        for source in range(1, sections):
            value = value + incoming[source].astype(F32)
        return value

    if channels % 128 == 0:

        def fill(step):
            target = lax.rem(section + step, sections)
            columns = pl.ds(pl.multiple_of(target * channels, channels), channels)
            one_out[target] = conv(taps, v_one, columns)

    else:
        partial = conv(taps, v_one)
        for target in range(sections):
            one_out[target] = partial[:, target * channels : (target + 1) * channels]

        def fill(step):
            pass

    arrivals, one_sent = exchange(0, lambda target: one_out.at[target], one_in, fill)
    fill(0)
    one_in[section] = one_out[section]
    arrivals()
    one = gelu(total(one_in)).astype(BF16)

    natural = 2 * two_rows
    order = (natural, one_rows)
    chosen = iota(order, 1) == (1 + iota(order, 0) % 2) * two_rows + iota(order, 0) // 2
    one_natural = dot(jnp.where(chosen, 1.0, 0.0).astype(BF16), one).astype(BF16)
    part_out[...] = dot_nt(own_head[...], one_natural)[0 : part_out.shape[0]]
    part_arrivals, part_sent = exchange(2, lambda target: part_out, part_in)
    two_out[...] = conv([one[block * two_rows : (block + 1) * two_rows] for block in range(3)], v_two)
    two_arrivals, two_sent = exchange(1, lambda target: two_out, two_in)
    two_in[section] = two_out[...]
    part_in[section] = part_out[...]
    one_sent()
    film_sent(1)
    two_arrivals()
    two = gelu(total(two_in)).astype(BF16)
    every_head = jnp.concatenate([all_head[source] for source in range(sections)], axis=1)
    level_two = dot_nt(two, every_head)
    part_arrivals()
    heads[0 : part_out.shape[0], 0:natural] = total(part_in)
    heads[own_head.shape[0] :, 0 : own_head.shape[0]] = level_two
    two_sent()
    part_sent()


def split_heads(heads, head_one, head_two):
    outputs, natural = head_one.shape
    two_rows = head_two.shape[0]
    head_one[...] = heads[0:outputs, 0:natural]
    head_two[...] = heads[heads.shape[0] - two_rows :, 0:outputs]


def on_device(
    patches,
    clip_slot,
    w_qkv,
    w_out,
    w_up,
    w_down,
    norm_gains,
    level_one_weight,
    level_two_weight,
    head_weight,
):
    sections = lax.axis_size("section")
    shards = lax.axis_size("dp")
    rows, channels = patches.shape
    width = channels * sections
    unit_rows = UNIT_ROWS
    units = rows // unit_rows
    tubes_unit = unit_rows // PATCHES
    outputs = head_weight.shape[1]
    one_rows = rows // PATCHES // 2
    two_rows = one_rows // 2
    vmem = pl.BlockSpec(memory_space=pltpu.VMEM)
    anywhere = pl.BlockSpec(memory_space=pl.ANY)
    dma = pltpu.SemaphoreType.DMA
    group = min(256, w_out.shape[1])
    part_rows = -(-outputs // 8) * 8
    head_rows = -(-outputs // 16) * 16
    heads = pl.pallas_call(
        functools.partial(kernel, sections, shards),
        out_shape=pltpu.VMEM((head_rows + two_rows, 128), F32),
        in_specs=[anywhere] * 10,
        out_specs=vmem,
        scratch_shapes=[
            pltpu.VMEM(w_qkv.shape[1:], BF16),
            pltpu.VMEM(w_out.shape[1:], BF16),
            pltpu.VMEM(w_up.shape[1:], BF16),
            pltpu.VMEM(w_down.shape[1:], BF16),
            pltpu.VMEM(level_one_weight.shape, BF16),
            pltpu.VMEM(level_two_weight.shape, BF16),
            pltpu.VMEM(patches.shape, BF16),
            pltpu.VMEM((units, sections, unit_rows, channels), BF16),
            pltpu.VMEM((units, sections, unit_rows, channels), BF16),
            pltpu.VMEM((sections, units * tubes_unit, channels), BF16),
            pltpu.VMEM((shards, units * tubes_unit, channels), BF16),
            pltpu.VMEM((sections, 3 * two_rows, channels), BF16),
            pltpu.VMEM((sections, 3 * two_rows, channels), BF16),
            pltpu.VMEM((two_rows, width), BF16),
            pltpu.VMEM((sections, two_rows, width), BF16),
            pltpu.VMEM((part_rows, 2 * two_rows), F32),
            pltpu.VMEM((sections, part_rows, 2 * two_rows), F32),
            pltpu.VMEM((head_rows, channels), BF16),
            pltpu.VMEM((sections, head_rows, channels), BF16),
            pltpu.VMEM((group, group), BF16),
            pltpu.VMEM((2 * unit_rows, 2 * HEAD), BF16),
            pltpu.VMEM((unit_rows, 2 * unit_rows), BF16),
            pltpu.VMEM((9 * two_rows, shards * units * tubes_unit), BF16),
            pltpu.VMEM((1, clip_slot.shape[0]), jnp.int32),
            pltpu.VMEM(norm_gains.shape, F32),
            pltpu.VMEM((outputs, channels), BF16),
            dma((10,)),
            dma((units,)),
            dma((units,)),
            dma((units,)),
            dma((2, sections, shards)),
            dma((2, shards)),
            dma((4, sections)),
            dma((4, sections)),
        ],
        compiler_params=pltpu.CompilerParams(
            collective_id=0, has_side_effects=True, vmem_limit_bytes=60 * 1024 * 1024
        ),
    )(
        patches,
        clip_slot.reshape(1, -1),
        w_qkv,
        w_out,
        w_up,
        w_down,
        norm_gains,
        level_one_weight,
        level_two_weight,
        head_weight.T,
    )
    head_one, head_two = pl.pallas_call(
        split_heads,
        out_shape=(
            jax.ShapeDtypeStruct((outputs, one_rows), F32),
            jax.ShapeDtypeStruct((two_rows, outputs), F32),
        ),
        in_specs=[vmem],
        out_specs=(vmem, vmem),
    )(pltpu.with_memory_space_constraint(heads, pltpu.VMEM))
    return head_one.T, head_two


def solution(mesh):
    return jax.shard_map(
        on_device,
        mesh=mesh,
        in_specs=(
            P(("groups", "dp"), "section"),
            P("groups"),
            P("section", None, None),
            P("section", None, None),
            P("section", None, None),
            P("section", None, None),
            P("section", None, None),
            P(None, "section", None),
            P(None, "section", None),
            P("section", None),
        ),
        out_specs=(P(("groups", "dp"), None), P(("groups", "dp"), None)),
        check_vma=False,
    )
```

```python
import functools

import jax
import jax.numpy as jnp
from jax import lax
from jax.experimental import pallas as pl
from jax.experimental.pallas import tpu as pltpu
from jax.sharding import PartitionSpec as P

HEADS = 8
HEAD = 64
PATCHES = 16
TUB_CLIP = 2
EPSILON = 1e-05
UNIT_ROWS = 128
ROW_BLOCK = 128
CHUNK = 512
COLUMNS = 256
MESH = pl.DeviceIdType.MESH
F32 = jnp.float32
BF16 = jnp.bfloat16


def dot(a, b):
    return jnp.dot(a, b, preferred_element_type=F32)


def dot_nt(a, b):
    return lax.dot_general(a, b, (((1,), (1,)), ((), ())), preferred_element_type=F32)


def gelu(values):
    return jax.nn.gelu(values, approximate=True)


def gelu_rounded(values):
    x = values.astype(BF16)
    inner = x * (x * x * 0.035677408136300125 + 0.7978845608028654)
    return x * (jnp.tanh(inner) * 0.5 + 0.5)


def iota(shape, dim):
    return lax.broadcasted_iota(jnp.int32, shape, dim)


def centre(values, scaling):
    width = values.shape[1]
    lanes = [values[:, start : start + 128] for start in range(0, width, 128)]
    sums = lanes[0]
    squares = lanes[0] * lanes[0]
    for lane in lanes[1:]:
        sums = sums + lane
        squares = squares + lane * lane
    average = jnp.sum(sums, axis=-1, keepdims=True) * (1.0 / width)
    square = jnp.sum(squares, axis=-1, keepdims=True) * (1.0 / width)
    spread = jnp.maximum(square - average * average, 0.0) + EPSILON
    return ((values - average) * scaling).astype(BF16), spread


def backbone_layer(stream, gains, v_qkv, v_out, v_up, averaging, own, clip_mask, emit):
    inner = v_out.shape[0]
    hidden = v_up.shape[1]
    pair = 2 * HEAD
    group = averaging.shape[0]
    normed, spread = centre(stream, gains[0, 0:1])
    raw = []
    for start in range(0, inner, group):
        raw.append(
            (
                dot(normed, v_qkv[:, start : start + group]),
                dot(normed, v_qkv[:, inner + start : inner + start + group]),
            )
        )
    floor = EPSILON * spread

    def head_scale(part):
        return part * lax.rsqrt(dot((part * part).astype(BF16), averaging[...]) + floor)

    scaled = [
        ((head_scale(raw_q) * HEAD**-0.5).astype(BF16), head_scale(raw_k).astype(BF16))
        for raw_q, raw_k in raw
    ]
    scale = lax.rsqrt(spread)
    values = [
        (dot(normed, v_qkv[:, 2 * inner + start : 2 * inner + start + group]) * scale).astype(BF16)
        for start in range(0, inner, group)
    ]
    scores = []
    stacked = []
    for (query, key), value in zip(scaled, values):
        for lane in range(0, group, pair):
            k = key[:, lane : lane + pair]
            v = value[:, lane : lane + pair]
            k2 = jnp.concatenate([k, k], axis=0) * own[...]
            v2 = jnp.concatenate([v, v], axis=0) * own[...]
            scores.append(dot_nt(query[:, lane : lane + pair], k2))
            stacked.append(jnp.concatenate([v2, own[...]], axis=1))
    weights = [jnp.exp(score).astype(BF16) * clip_mask[...] for score in scores]
    mixed = []
    for weight, stack in zip(weights, stacked):
        both = dot(weight, stack)
        mixed.append((both[:, :pair] / both[:, pair:]).astype(BF16))
    residual = stream + dot(jnp.concatenate(mixed, axis=1), v_out[...])
    normed_b, spread_b = centre(residual, gains[0, 1:2])
    scale_b = lax.rsqrt(spread_b)
    parts = [
        gelu_rounded(dot(normed_b, v_up[:, start : start + CHUNK]) * scale_b)
        for start in range(0, hidden, CHUNK)
    ]
    emit(residual, jnp.concatenate(parts, axis=1))


def kernel(
    sections,
    shards,
    patches,
    slot_in,
    w_qkv,
    w_out,
    w_up,
    w_down,
    gains_in,
    one_weight,
    two_weight,
    head_in,
    heads,
    v_qkv,
    v_out,
    v_up,
    v_down,
    v_one,
    v_two,
    patch_buf,
    inbuf,
    outbuf,
    pooled_out,
    film_in,
    one_out,
    one_in,
    two_out,
    two_in,
    part_out,
    part_in,
    own_head,
    all_head,
    averaging,
    own,
    clip_mask,
    selector,
    clip_slot,
    gains,
    head_weight,
    weight_sem,
    gather_send,
    arrive,
    hop_send,
    film_send,
    film_recv,
    ex_send,
    ex_recv,
):
    section = lax.axis_index("section")
    shard = lax.axis_index("dp")
    last = sections - 1
    units, _, unit_rows, channels = outbuf.shape
    width = sections * channels
    tubes_unit = unit_rows // PATCHES
    outputs = head_weight.shape[0]
    loads = [
        pltpu.make_async_copy(source, target, weight_sem.at[index])
        for index, (source, target) in enumerate(
            (
                (w_qkv.at[0], v_qkv),
                (w_out.at[0], v_out),
                (w_up.at[0], v_up),
                (w_down.at[0], v_down),
                (one_weight, v_one),
                (two_weight, v_two),
            )
        )
    ]
    def each_unit(body):
        def step(u, carry):
            body(u)
            return carry

        lax.fori_loop(0, units, step, 0)

    def patch_rows(u):
        return pl.ds(pl.multiple_of(u * unit_rows, unit_rows), unit_rows)

    patch_load = pltpu.make_async_copy(patches, patch_buf, weight_sem.at[6])

    @pl.when(section > 0)
    def _():
        patch_load.start()

    @pl.when(section == 0)
    def _():
        each_unit(
            lambda u: pltpu.make_async_copy(
                patches.at[patch_rows(u)], inbuf.at[u, 0], arrive.at[u]
            ).start()
        )

    small = [
        pltpu.make_async_copy(source, target, weight_sem.at[7 + index])
        for index, (source, target) in enumerate(
            ((slot_in, clip_slot), (gains_in, gains), (head_in, head_weight))
        )
    ]
    for load in small + loads[:4]:
        load.start()

    same = iota(averaging.shape, 0) // HEAD == iota(averaging.shape, 1) // HEAD
    averaging[...] = jnp.where(same, 1.0 / HEAD, 0.0).astype(BF16)
    mine = (iota(own.shape, 0) < unit_rows) == (iota(own.shape, 1) < HEAD)
    own[...] = jnp.where(mine, 1.0, 0.0).astype(BF16)
    clip = PATCHES * TUB_CLIP
    same_clip = iota(clip_mask.shape, 0) // clip == iota(clip_mask.shape, 1) % unit_rows // clip
    clip_mask[...] = jnp.where(same_clip, 1.0, 0.0).astype(BF16)

    barrier = pltpu.get_barrier_semaphore()
    for ds in range(sections):
        for dd in range(shards):
            if ds or dd:
                pl.semaphore_signal(
                    barrier,
                    inc=1,
                    device_id={
                        "section": lax.rem(section + ds, sections),
                        "dp": lax.rem(shard + dd, shards),
                    },
                    device_id_type=MESH,
                )
    pl.semaphore_wait(barrier, sections * shards - 1)

    def patch_copy(u):
        return pltpu.make_async_remote_copy(
            src_ref=patch_buf.at[patch_rows(u)],
            dst_ref=inbuf.at[u, section],
            send_sem=gather_send.at[u],
            recv_sem=arrive.at[u],
            device_id={"section": 0},
            device_id_type=MESH,
        )

    @pl.when(section > 0)
    def _():
        patch_load.wait()
        each_unit(lambda u: patch_copy(u).start())

    def hop(u):
        return pltpu.make_async_remote_copy(
            src_ref=outbuf.at[u],
            dst_ref=inbuf.at[u],
            send_sem=hop_send.at[u],
            recv_sem=arrive.at[u],
            device_id={"section": lax.rem(section + 1, sections)},
            device_id_type=MESH,
        )

    def arrival(slot):
        return pltpu.make_async_copy(inbuf.at[slot], inbuf.at[slot], arrive.at[slot])

    tubes_own = units * tubes_unit
    tubes_pair = 2 * tubes_unit
    batches = ((0, tubes_own - tubes_pair), (tubes_own - tubes_pair, tubes_pair))
    film_targets = [
        (target, step)
        for target in range(sections)
        for step in range(shards)
        if not (target == last and step == 0)
    ]

    def film_copy(batch, target, step):
        start, count = batches[batch]
        return pltpu.make_async_remote_copy(
            src_ref=pooled_out.at[target, pl.ds(start, count)],
            dst_ref=film_in.at[shard, pl.ds(start, count)],
            send_sem=film_send.at[batch, target, step],
            recv_sem=film_recv.at[batch, shard],
            device_id={"section": target, "dp": lax.rem(shard + step, shards)},
            device_id_type=MESH,
        )

    def film_arrival(batch, source):
        start, count = batches[batch]
        return pltpu.make_async_copy(
            film_in.at[source, pl.ds(start, count)],
            film_in.at[source, pl.ds(start, count)],
            film_recv.at[batch, source],
        )

    pooling_shape = (tubes_pair, 2 * unit_rows)
    pooling = jnp.where(
        iota(pooling_shape, 1) // PATCHES == iota(pooling_shape, 0), 1.0 / PATCHES, 0.0
    ).astype(BF16)

    def pool(p, send=None):
        rows = pl.ds(pl.multiple_of(p * tubes_pair, tubes_pair), tubes_pair)
        for target in range(sections):
            both = jnp.concatenate([outbuf[2 * p, target], outbuf[2 * p + 1, target]], axis=0)
            pooled = dot(pooling, both).astype(BF16)
            pooled_out[target, rows] = pooled
            if target == last:
                film_in[shard, rows] = pooled
            if send is not None:
                send(target)

    def exchange(stage, outgoing, incoming, fill=None):
        copies = []
        for step in range(sections - 1, 0, -1):
            if fill is not None:
                fill(step)
            target = lax.rem(section + step, sections)
            copies.append(
                pltpu.make_async_remote_copy(
                    src_ref=outgoing(target),
                    dst_ref=incoming.at[section],
                    send_sem=ex_send.at[stage, step],
                    recv_sem=ex_recv.at[stage, section],
                    device_id={"section": target},
                    device_id_type=MESH,
                )
            )
            copies[-1].start()

        def arrivals():
            for step in range(1, sections):
                source = lax.rem(section + step, sections)
                pltpu.make_async_copy(
                    incoming.at[source], incoming.at[source], ex_recv.at[stage, source]
                ).wait()

        def sent():
            for copy in copies:
                copy.wait_send()

        return arrivals, sent

    for load in small:
        load.wait()
    own_head[...] = jnp.zeros(own_head.shape, BF16)
    own_head[0:outputs] = head_weight[...]
    head_arrivals, head_sent = exchange(3, lambda target: own_head, all_head)
    all_head[section] = own_head[...]

    tubes = selector.shape[1]
    clips = tubes // TUB_CLIP
    spread_shape = (clips, tubes)
    spread = jnp.where(iota(spread_shape, 1) // TUB_CLIP == iota(spread_shape, 0), 1.0, 0.0)
    slots = jnp.broadcast_to(clip_slot[...].astype(F32), (8, clips)).astype(BF16)
    position = TUB_CLIP * dot(slots, spread.astype(BF16))[0:1]
    position = position + (iota((1, tubes), 1) % TUB_CLIP).astype(F32)
    two_rows = two_out.shape[0]
    one_rows = 3 * two_rows
    row = iota((one_rows, 1), 0)
    level_index = 2 * (shard * two_rows + row % two_rows) + row // two_rows - 1
    for tap in range(3):
        wanted = (2 * level_index + tap - 1).astype(F32)
        chosen = jnp.where(position == wanted, 1.0, 0.0).astype(BF16)
        selector[tap * one_rows : (tap + 1) * one_rows] = chosen

    for load in loads[:4]:
        load.wait()
    for load in loads[4:]:
        load.start()

    blocks = max(1, COLUMNS // channels)

    def run_unit(u):
        arrival(u).wait()
        stream = jnp.concatenate([inbuf[u, source] for source in range(sections)], axis=1)

        def emit(residual, gated):
            for first in range(0, sections, blocks):
                columns = slice(first * channels, (first + blocks) * channels)
                result = (residual[:, columns] + dot(gated, v_down[:, columns])).astype(BF16)
                for block in range(blocks):
                    outbuf[u, first + block] = result[:, block * channels : (block + 1) * channels]

        backbone_layer(
            stream.astype(F32), gains, v_qkv, v_out, v_up, averaging, own, clip_mask, emit
        )

        @pl.when(section < last)
        def _():
            hop(u).start()

        def film_start(batch, chosen):
            for target, step in film_targets:
                if target == chosen:
                    film_copy(batch, target, step).start()

        @pl.when((section == last) & (u % 2 == 1) & (u < units - 1))
        def _():
            pool(u // 2)

            @pl.when(u == units - 3)
            def _():
                for target in range(sections):
                    film_start(0, target)

        @pl.when((section == last) & (u == units - 1))
        def _():
            pool(u // 2, lambda target: film_start(1, target))

    each_unit(run_unit)

    def film_sent(batch):
        @pl.when(section == last)
        def _():
            for target, step in film_targets:
                film_copy(batch, target, step).wait_send()

    def finish():
        head_arrivals()
        head_sent()

        @pl.when(section > 0)
        def _():
            each_unit(lambda u: patch_copy(u).wait_send())

        @pl.when(section < last)
        def _():
            each_unit(lambda u: hop(u).wait_send())

        film_sent(0)

    loads[4].wait()
    loads[5].wait()
    finish()

    for batch in (0, 1):

        @pl.when(section < last)
        def _():
            film_arrival(batch, shard).wait()

        for step in range(1, shards):
            film_arrival(batch, lax.rem(shard + step, shards)).wait()

    pooled = film_in[...].reshape(tubes, channels)
    picked = dot(selector[...], pooled).astype(BF16)
    taps = [picked[tap * one_rows : (tap + 1) * one_rows] for tap in range(3)]

    def conv(parts, weight, columns=slice(None)):
        total = dot(parts[0], weight[0, :, columns])
        for tap in (1, 2):
            total = total + dot(parts[tap], weight[tap, :, columns])
        return total.astype(BF16)

    def total(incoming):
        value = incoming[0].astype(F32)
        for source in range(1, sections):
            value = value + incoming[source].astype(F32)
        return value

    if channels % 128 == 0:

        def fill(step):
            target = lax.rem(section + step, sections)
            columns = pl.ds(pl.multiple_of(target * channels, channels), channels)
            one_out[target] = conv(taps, v_one, columns)

    else:
        partial = conv(taps, v_one)
        for target in range(sections):
            one_out[target] = partial[:, target * channels : (target + 1) * channels]

        def fill(step):
            pass

    arrivals, one_sent = exchange(0, lambda target: one_out.at[target], one_in, fill)
    fill(0)
    one_in[section] = one_out[section]
    arrivals()
    one = gelu(total(one_in)).astype(BF16)

    two_out[...] = conv([one[block * two_rows : (block + 1) * two_rows] for block in range(3)], v_two)
    two_arrivals, two_sent = exchange(1, lambda target: two_out, two_in)
    natural = 2 * two_rows
    order = (natural, one_rows)
    chosen = iota(order, 1) == (1 + iota(order, 0) % 2) * two_rows + iota(order, 0) // 2
    one_natural = dot(jnp.where(chosen, 1.0, 0.0).astype(BF16), one).astype(BF16)
    part_out[...] = dot_nt(own_head[...], one_natural)[0 : part_out.shape[0]]
    part_arrivals, part_sent = exchange(2, lambda target: part_out, part_in)
    two_in[section] = two_out[...]
    part_in[section] = part_out[...]
    one_sent()
    film_sent(1)
    two_arrivals()
    two = gelu(total(two_in)).astype(BF16)
    every_head = jnp.concatenate([all_head[source] for source in range(sections)], axis=1)
    level_two = dot_nt(two, every_head)
    part_arrivals()
    heads[0 : part_out.shape[0], 0:natural] = total(part_in)
    heads[own_head.shape[0] :, 0 : own_head.shape[0]] = level_two
    two_sent()
    part_sent()


def split_heads(heads, head_one, head_two):
    outputs, natural = head_one.shape
    two_rows = head_two.shape[0]
    head_one[...] = heads[0:outputs, 0:natural]
    head_two[...] = heads[heads.shape[0] - two_rows :, 0:outputs]


def on_device(
    patches,
    clip_slot,
    w_qkv,
    w_out,
    w_up,
    w_down,
    norm_gains,
    level_one_weight,
    level_two_weight,
    head_weight,
):
    sections = lax.axis_size("section")
    shards = lax.axis_size("dp")
    rows, channels = patches.shape
    width = channels * sections
    unit_rows = UNIT_ROWS
    units = rows // unit_rows
    tubes_unit = unit_rows // PATCHES
    outputs = head_weight.shape[1]
    one_rows = rows // PATCHES // 2
    two_rows = one_rows // 2
    vmem = pl.BlockSpec(memory_space=pltpu.VMEM)
    anywhere = pl.BlockSpec(memory_space=pl.ANY)
    dma = pltpu.SemaphoreType.DMA
    group = min(256, w_out.shape[1])
    part_rows = -(-outputs // 8) * 8
    head_rows = -(-outputs // 16) * 16
    heads = pl.pallas_call(
        functools.partial(kernel, sections, shards),
        out_shape=pltpu.VMEM((head_rows + two_rows, 128), F32),
        in_specs=[anywhere] * 10,
        out_specs=vmem,
        scratch_shapes=[
            pltpu.VMEM(w_qkv.shape[1:], BF16),
            pltpu.VMEM(w_out.shape[1:], BF16),
            pltpu.VMEM(w_up.shape[1:], BF16),
            pltpu.VMEM(w_down.shape[1:], BF16),
            pltpu.VMEM(level_one_weight.shape, BF16),
            pltpu.VMEM(level_two_weight.shape, BF16),
            pltpu.VMEM(patches.shape, BF16),
            pltpu.VMEM((units, sections, unit_rows, channels), BF16),
            pltpu.VMEM((units, sections, unit_rows, channels), BF16),
            pltpu.VMEM((sections, units * tubes_unit, channels), BF16),
            pltpu.VMEM((shards, units * tubes_unit, channels), BF16),
            pltpu.VMEM((sections, 3 * two_rows, channels), BF16),
            pltpu.VMEM((sections, 3 * two_rows, channels), BF16),
            pltpu.VMEM((two_rows, width), BF16),
            pltpu.VMEM((sections, two_rows, width), BF16),
            pltpu.VMEM((part_rows, 2 * two_rows), F32),
            pltpu.VMEM((sections, part_rows, 2 * two_rows), F32),
            pltpu.VMEM((head_rows, channels), BF16),
            pltpu.VMEM((sections, head_rows, channels), BF16),
            pltpu.VMEM((group, group), BF16),
            pltpu.VMEM((2 * unit_rows, 2 * HEAD), BF16),
            pltpu.VMEM((unit_rows, 2 * unit_rows), BF16),
            pltpu.VMEM((9 * two_rows, shards * units * tubes_unit), BF16),
            pltpu.VMEM((1, clip_slot.shape[0]), jnp.int32),
            pltpu.VMEM(norm_gains.shape, F32),
            pltpu.VMEM((outputs, channels), BF16),
            dma((10,)),
            dma((units,)),
            dma((units,)),
            dma((units,)),
            dma((2, sections, shards)),
            dma((2, shards)),
            dma((4, sections)),
            dma((4, sections)),
        ],
        compiler_params=pltpu.CompilerParams(
            collective_id=0, has_side_effects=True, vmem_limit_bytes=60 * 1024 * 1024
        ),
    )(
        patches,
        clip_slot.reshape(1, -1),
        w_qkv,
        w_out,
        w_up,
        w_down,
        norm_gains,
        level_one_weight,
        level_two_weight,
        head_weight.T,
    )
    head_one, head_two = pl.pallas_call(
        split_heads,
        out_shape=(
            jax.ShapeDtypeStruct((outputs, one_rows), F32),
            jax.ShapeDtypeStruct((two_rows, outputs), F32),
        ),
        in_specs=[vmem],
        out_specs=(vmem, vmem),
    )(pltpu.with_memory_space_constraint(heads, pltpu.VMEM))
    return head_one.T, head_two


def solution(mesh):
    return jax.shard_map(
        on_device,
        mesh=mesh,
        in_specs=(
            P(("groups", "dp"), "section"),
            P("groups"),
            P("section", None, None),
            P("section", None, None),
            P("section", None, None),
            P("section", None, None),
            P("section", None, None),
            P(None, "section", None),
            P(None, "section", None),
            P("section", None),
        ),
        out_specs=(P(("groups", "dp"), None), P(("groups", "dp"), None)),
        check_vma=False,
    )
```

```python
import functools

import jax
import jax.numpy as jnp
from jax import lax
from jax.experimental import pallas as pl
from jax.experimental.pallas import tpu as pltpu
from jax.sharding import PartitionSpec as P

HEADS = 8
HEAD = 64
PATCHES = 16
TUB_CLIP = 2
EPSILON = 1e-05
UNIT_ROWS = 128
ROW_BLOCK = 128
CHUNK = 512
COLUMNS = 256
MESH = pl.DeviceIdType.MESH
F32 = jnp.float32
BF16 = jnp.bfloat16


def dot(a, b):
    return jnp.dot(a, b, preferred_element_type=F32)


def dot_nt(a, b):
    return lax.dot_general(a, b, (((1,), (1,)), ((), ())), preferred_element_type=F32)


def gelu(values):
    return jax.nn.gelu(values, approximate=True)


def gelu_rounded(values):
    x = values.astype(BF16)
    inner = x * (x * x * 0.035677408136300125 + 0.7978845608028654)
    return x * (jnp.tanh(inner) * 0.5 + 0.5)


def iota(shape, dim):
    return lax.broadcasted_iota(jnp.int32, shape, dim)


def centre(values, scaling):
    width = values.shape[1]
    lanes = [values[:, start : start + 128] for start in range(0, width, 128)]
    sums = lanes[0]
    squares = lanes[0] * lanes[0]
    for lane in lanes[1:]:
        sums = sums + lane
        squares = squares + lane * lane
    average = jnp.sum(sums, axis=-1, keepdims=True) * (1.0 / width)
    square = jnp.sum(squares, axis=-1, keepdims=True) * (1.0 / width)
    spread = jnp.maximum(square - average * average, 0.0) + EPSILON
    return ((values - average) * scaling).astype(BF16), spread


def backbone_layer(stream, gains, v_qkv, v_out, v_up, averaging, own, clip_mask, emit):
    inner = v_out.shape[0]
    hidden = v_up.shape[1]
    pair = 2 * HEAD
    group = averaging.shape[0]
    normed, spread = centre(stream, gains[0, 0:1])
    raw = []
    for start in range(0, inner, group):
        raw.append(
            (
                dot(normed, v_qkv[:, start : start + group]),
                dot(normed, v_qkv[:, inner + start : inner + start + group]),
            )
        )
    floor = EPSILON * spread

    def head_scale(part):
        return part * lax.rsqrt(dot((part * part).astype(BF16), averaging[...]) + floor)

    scaled = [
        ((head_scale(raw_q) * HEAD**-0.5).astype(BF16), head_scale(raw_k).astype(BF16))
        for raw_q, raw_k in raw
    ]
    scale = lax.rsqrt(spread)
    values = [
        (dot(normed, v_qkv[:, 2 * inner + start : 2 * inner + start + group]) * scale).astype(BF16)
        for start in range(0, inner, group)
    ]
    scores = []
    stacked = []
    for (query, key), value in zip(scaled, values):
        for lane in range(0, group, pair):
            k = key[:, lane : lane + pair]
            v = value[:, lane : lane + pair]
            k2 = jnp.concatenate([k, k], axis=0) * own[...]
            v2 = jnp.concatenate([v, v], axis=0) * own[...]
            scores.append(dot_nt(query[:, lane : lane + pair], k2))
            stacked.append(jnp.concatenate([v2, own[...]], axis=1))
    weights = [jnp.exp(score).astype(BF16) * clip_mask[...] for score in scores]
    mixed = []
    for weight, stack in zip(weights, stacked):
        both = dot(weight, stack)
        mixed.append((both[:, :pair] / both[:, pair:]).astype(BF16))
    residual = stream + dot(jnp.concatenate(mixed, axis=1), v_out[...])
    normed_b, spread_b = centre(residual, gains[0, 1:2])
    scale_b = lax.rsqrt(spread_b)
    parts = [
        gelu_rounded(dot(normed_b, v_up[:, start : start + CHUNK]) * scale_b)
        for start in range(0, hidden, CHUNK)
    ]
    emit(residual, jnp.concatenate(parts, axis=1))


def kernel(
    sections,
    shards,
    patches,
    slot_in,
    w_qkv,
    w_out,
    w_up,
    w_down,
    gains_in,
    one_weight,
    two_weight,
    head_in,
    heads,
    v_qkv,
    v_out,
    v_up,
    v_down,
    v_one,
    v_two,
    patch_buf,
    inbuf,
    outbuf,
    pooled_out,
    film_in,
    one_out,
    one_in,
    two_out,
    two_in,
    part_out,
    part_in,
    own_head,
    all_head,
    averaging,
    own,
    clip_mask,
    selector,
    clip_slot,
    gains,
    head_weight,
    weight_sem,
    gather_send,
    arrive,
    hop_send,
    film_send,
    film_recv,
    ex_send,
    ex_recv,
):
    section = lax.axis_index("section")
    shard = lax.axis_index("dp")
    last = sections - 1
    units, _, unit_rows, channels = outbuf.shape
    width = sections * channels
    tubes_unit = unit_rows // PATCHES
    outputs = head_weight.shape[0]
    barrier = pltpu.get_barrier_semaphore()
    for ds in range(sections):
        for dd in range(shards):
            if ds or dd:
                pl.semaphore_signal(
                    barrier,
                    inc=1,
                    device_id={
                        "section": lax.rem(section + ds, sections),
                        "dp": lax.rem(shard + dd, shards),
                    },
                    device_id_type=MESH,
                )
    loads = [
        pltpu.make_async_copy(source, target, weight_sem.at[index])
        for index, (source, target) in enumerate(
            (
                (w_qkv.at[0], v_qkv),
                (w_out.at[0], v_out),
                (w_up.at[0], v_up),
                (w_down.at[0], v_down),
                (one_weight, v_one),
                (two_weight, v_two),
            )
        )
    ]
    def each_unit(body):
        def step(u, carry):
            body(u)
            return carry

        lax.fori_loop(0, units, step, 0)

    def patch_rows(u):
        return pl.ds(pl.multiple_of(u * unit_rows, unit_rows), unit_rows)

    patch_load = pltpu.make_async_copy(patches, patch_buf, weight_sem.at[6])

    @pl.when(section > 0)
    def _():
        patch_load.start()

    @pl.when(section == 0)
    def _():
        each_unit(
            lambda u: pltpu.make_async_copy(
                patches.at[patch_rows(u)], inbuf.at[u, 0], arrive.at[u]
            ).start()
        )

    small = [
        pltpu.make_async_copy(source, target, weight_sem.at[7 + index])
        for index, (source, target) in enumerate(
            ((slot_in, clip_slot), (gains_in, gains), (head_in, head_weight))
        )
    ]
    for load in small + loads[:4]:
        load.start()

    same = iota(averaging.shape, 0) // HEAD == iota(averaging.shape, 1) // HEAD
    averaging[...] = jnp.where(same, 1.0 / HEAD, 0.0).astype(BF16)
    mine = (iota(own.shape, 0) < unit_rows) == (iota(own.shape, 1) < HEAD)
    own[...] = jnp.where(mine, 1.0, 0.0).astype(BF16)
    clip = PATCHES * TUB_CLIP
    same_clip = iota(clip_mask.shape, 0) // clip == iota(clip_mask.shape, 1) % unit_rows // clip
    clip_mask[...] = jnp.where(same_clip, 1.0, 0.0).astype(BF16)

    pl.semaphore_wait(barrier, sections * shards - 1)

    def patch_copy(u):
        return pltpu.make_async_remote_copy(
            src_ref=patch_buf.at[patch_rows(u)],
            dst_ref=inbuf.at[u, section],
            send_sem=gather_send.at[u],
            recv_sem=arrive.at[u],
            device_id={"section": 0},
            device_id_type=MESH,
        )

    @pl.when(section > 0)
    def _():
        patch_load.wait()
        each_unit(lambda u: patch_copy(u).start())

    def hop(u):
        return pltpu.make_async_remote_copy(
            src_ref=outbuf.at[u],
            dst_ref=inbuf.at[u],
            send_sem=hop_send.at[u],
            recv_sem=arrive.at[u],
            device_id={"section": lax.rem(section + 1, sections)},
            device_id_type=MESH,
        )

    def arrival(slot):
        return pltpu.make_async_copy(inbuf.at[slot], inbuf.at[slot], arrive.at[slot])

    tubes_own = units * tubes_unit
    tubes_pair = 2 * tubes_unit
    batches = ((0, tubes_own - tubes_pair), (tubes_own - tubes_pair, tubes_pair))
    film_targets = [
        (target, step)
        for target in range(sections)
        for step in range(shards)
        if not (target == last and step == 0)
    ]

    def film_copy(batch, target, step):
        start, count = batches[batch]
        return pltpu.make_async_remote_copy(
            src_ref=pooled_out.at[target, pl.ds(start, count)],
            dst_ref=film_in.at[shard, pl.ds(start, count)],
            send_sem=film_send.at[batch, target, step],
            recv_sem=film_recv.at[batch, shard],
            device_id={"section": target, "dp": lax.rem(shard + step, shards)},
            device_id_type=MESH,
        )

    def film_arrival(batch, source):
        start, count = batches[batch]
        return pltpu.make_async_copy(
            film_in.at[source, pl.ds(start, count)],
            film_in.at[source, pl.ds(start, count)],
            film_recv.at[batch, source],
        )

    pooling_shape = (tubes_pair, 2 * unit_rows)
    pooling = jnp.where(
        iota(pooling_shape, 1) // PATCHES == iota(pooling_shape, 0), 1.0 / PATCHES, 0.0
    ).astype(BF16)

    def pool(p, send=None):
        rows = pl.ds(pl.multiple_of(p * tubes_pair, tubes_pair), tubes_pair)
        for target in range(sections):
            both = jnp.concatenate([outbuf[2 * p, target], outbuf[2 * p + 1, target]], axis=0)
            pooled = dot(pooling, both).astype(BF16)
            pooled_out[target, rows] = pooled
            if target == last:
                film_in[shard, rows] = pooled
            if send is not None:
                send(target)

    def exchange(stage, outgoing, incoming, fill=None):
        copies = []
        for step in range(sections - 1, 0, -1):
            if fill is not None:
                fill(step)
            target = lax.rem(section + step, sections)
            copies.append(
                pltpu.make_async_remote_copy(
                    src_ref=outgoing(target),
                    dst_ref=incoming.at[section],
                    send_sem=ex_send.at[stage, step],
                    recv_sem=ex_recv.at[stage, section],
                    device_id={"section": target},
                    device_id_type=MESH,
                )
            )
            copies[-1].start()

        def arrivals():
            for step in range(1, sections):
                source = lax.rem(section + step, sections)
                pltpu.make_async_copy(
                    incoming.at[source], incoming.at[source], ex_recv.at[stage, source]
                ).wait()

        def sent():
            for copy in copies:
                copy.wait_send()

        return arrivals, sent

    for load in small:
        load.wait()
    own_head[...] = jnp.zeros(own_head.shape, BF16)
    own_head[0:outputs] = head_weight[...]
    head_arrivals, head_sent = exchange(3, lambda target: own_head, all_head)
    all_head[section] = own_head[...]

    tubes = selector.shape[1]
    clips = tubes // TUB_CLIP
    spread_shape = (clips, tubes)
    spread = jnp.where(iota(spread_shape, 1) // TUB_CLIP == iota(spread_shape, 0), 1.0, 0.0)
    slots = jnp.broadcast_to(clip_slot[...].astype(F32), (8, clips)).astype(BF16)
    position = TUB_CLIP * dot(slots, spread.astype(BF16))[0:1]
    position = position + (iota((1, tubes), 1) % TUB_CLIP).astype(F32)
    two_rows = two_out.shape[0]
    one_rows = 3 * two_rows
    row = iota((one_rows, 1), 0)
    level_index = 2 * (shard * two_rows + row % two_rows) + row // two_rows - 1
    for tap in range(3):
        wanted = (2 * level_index + tap - 1).astype(F32)
        chosen = jnp.where(position == wanted, 1.0, 0.0).astype(BF16)
        selector[tap * one_rows : (tap + 1) * one_rows] = chosen

    for load in loads[:4]:
        load.wait()
    for load in loads[4:]:
        load.start()

    blocks = max(1, COLUMNS // channels)

    def run_unit(u):
        arrival(u).wait()
        stream = jnp.concatenate([inbuf[u, source] for source in range(sections)], axis=1)

        def emit(residual, gated):
            for first in range(0, sections, blocks):
                columns = slice(first * channels, (first + blocks) * channels)
                result = (residual[:, columns] + dot(gated, v_down[:, columns])).astype(BF16)
                for block in range(blocks):
                    outbuf[u, first + block] = result[:, block * channels : (block + 1) * channels]

        backbone_layer(
            stream.astype(F32), gains, v_qkv, v_out, v_up, averaging, own, clip_mask, emit
        )

        @pl.when(section < last)
        def _():
            hop(u).start()

        def film_start(batch, chosen):
            for target, step in film_targets:
                if target == chosen:
                    film_copy(batch, target, step).start()

        @pl.when((section == last) & (u % 2 == 1) & (u < units - 1))
        def _():
            pool(u // 2)

            @pl.when(u == units - 3)
            def _():
                for target in range(sections):
                    film_start(0, target)

        @pl.when((section == last) & (u == units - 1))
        def _():
            pool(u // 2, lambda target: film_start(1, target))

    each_unit(run_unit)

    def film_sent(batch):
        @pl.when(section == last)
        def _():
            for target, step in film_targets:
                film_copy(batch, target, step).wait_send()

    def finish():
        head_arrivals()
        head_sent()

        @pl.when(section > 0)
        def _():
            each_unit(lambda u: patch_copy(u).wait_send())

        @pl.when(section < last)
        def _():
            each_unit(lambda u: hop(u).wait_send())

        film_sent(0)

    loads[4].wait()
    loads[5].wait()
    finish()

    for batch in (0, 1):

        @pl.when(section < last)
        def _():
            film_arrival(batch, shard).wait()

        for step in range(1, shards):
            film_arrival(batch, lax.rem(shard + step, shards)).wait()

    pooled = film_in[...].reshape(tubes, channels)
    picked = dot(selector[...], pooled).astype(BF16)
    taps = [picked[tap * one_rows : (tap + 1) * one_rows] for tap in range(3)]

    def conv(parts, weight, columns=slice(None)):
        total = dot(parts[0], weight[0, :, columns])
        for tap in (1, 2):
            total = total + dot(parts[tap], weight[tap, :, columns])
        return total.astype(BF16)

    def total(incoming):
        value = incoming[0].astype(F32)
        for source in range(1, sections):
            value = value + incoming[source].astype(F32)
        return value

    if channels % 128 == 0:

        def fill(step):
            target = lax.rem(section + step, sections)
            columns = pl.ds(pl.multiple_of(target * channels, channels), channels)
            one_out[target] = conv(taps, v_one, columns)

    else:
        partial = conv(taps, v_one)
        for target in range(sections):
            one_out[target] = partial[:, target * channels : (target + 1) * channels]

        def fill(step):
            pass

    arrivals, one_sent = exchange(0, lambda target: one_out.at[target], one_in, fill)
    fill(0)
    one_in[section] = one_out[section]
    arrivals()
    one = gelu(total(one_in)).astype(BF16)

    two_out[...] = conv([one[block * two_rows : (block + 1) * two_rows] for block in range(3)], v_two)
    two_arrivals, two_sent = exchange(1, lambda target: two_out, two_in)
    natural = 2 * two_rows
    order = (natural, one_rows)
    chosen = iota(order, 1) == (1 + iota(order, 0) % 2) * two_rows + iota(order, 0) // 2
    one_natural = dot(jnp.where(chosen, 1.0, 0.0).astype(BF16), one).astype(BF16)
    part_out[...] = dot_nt(own_head[...], one_natural)[0 : part_out.shape[0]]
    part_arrivals, part_sent = exchange(2, lambda target: part_out, part_in)
    two_in[section] = two_out[...]
    part_in[section] = part_out[...]
    one_sent()
    film_sent(1)
    two_arrivals()
    two = gelu(total(two_in)).astype(BF16)
    every_head = jnp.concatenate([all_head[source] for source in range(sections)], axis=1)
    level_two = dot_nt(two, every_head)
    part_arrivals()
    heads[0 : part_out.shape[0], 0:natural] = total(part_in)
    heads[own_head.shape[0] :, 0 : own_head.shape[0]] = level_two
    two_sent()
    part_sent()


def split_heads(heads, head_one, head_two):
    outputs, natural = head_one.shape
    two_rows = head_two.shape[0]
    head_one[...] = heads[0:outputs, 0:natural]
    head_two[...] = heads[heads.shape[0] - two_rows :, 0:outputs]


def on_device(
    patches,
    clip_slot,
    w_qkv,
    w_out,
    w_up,
    w_down,
    norm_gains,
    level_one_weight,
    level_two_weight,
    head_weight,
):
    sections = lax.axis_size("section")
    shards = lax.axis_size("dp")
    rows, channels = patches.shape
    width = channels * sections
    unit_rows = UNIT_ROWS
    units = rows // unit_rows
    tubes_unit = unit_rows // PATCHES
    outputs = head_weight.shape[1]
    one_rows = rows // PATCHES // 2
    two_rows = one_rows // 2
    vmem = pl.BlockSpec(memory_space=pltpu.VMEM)
    anywhere = pl.BlockSpec(memory_space=pl.ANY)
    dma = pltpu.SemaphoreType.DMA
    group = min(256, w_out.shape[1])
    part_rows = -(-outputs // 8) * 8
    head_rows = -(-outputs // 16) * 16
    heads = pl.pallas_call(
        functools.partial(kernel, sections, shards),
        out_shape=pltpu.VMEM((head_rows + two_rows, 128), F32),
        in_specs=[anywhere] * 10,
        out_specs=vmem,
        scratch_shapes=[
            pltpu.VMEM(w_qkv.shape[1:], BF16),
            pltpu.VMEM(w_out.shape[1:], BF16),
            pltpu.VMEM(w_up.shape[1:], BF16),
            pltpu.VMEM(w_down.shape[1:], BF16),
            pltpu.VMEM(level_one_weight.shape, BF16),
            pltpu.VMEM(level_two_weight.shape, BF16),
            pltpu.VMEM(patches.shape, BF16),
            pltpu.VMEM((units, sections, unit_rows, channels), BF16),
            pltpu.VMEM((units, sections, unit_rows, channels), BF16),
            pltpu.VMEM((sections, units * tubes_unit, channels), BF16),
            pltpu.VMEM((shards, units * tubes_unit, channels), BF16),
            pltpu.VMEM((sections, 3 * two_rows, channels), BF16),
            pltpu.VMEM((sections, 3 * two_rows, channels), BF16),
            pltpu.VMEM((two_rows, width), BF16),
            pltpu.VMEM((sections, two_rows, width), BF16),
            pltpu.VMEM((part_rows, 2 * two_rows), F32),
            pltpu.VMEM((sections, part_rows, 2 * two_rows), F32),
            pltpu.VMEM((head_rows, channels), BF16),
            pltpu.VMEM((sections, head_rows, channels), BF16),
            pltpu.VMEM((group, group), BF16),
            pltpu.VMEM((2 * unit_rows, 2 * HEAD), BF16),
            pltpu.VMEM((unit_rows, 2 * unit_rows), BF16),
            pltpu.VMEM((9 * two_rows, shards * units * tubes_unit), BF16),
            pltpu.VMEM((1, clip_slot.shape[0]), jnp.int32),
            pltpu.VMEM(norm_gains.shape, F32),
            pltpu.VMEM((outputs, channels), BF16),
            dma((10,)),
            dma((units,)),
            dma((units,)),
            dma((units,)),
            dma((2, sections, shards)),
            dma((2, shards)),
            dma((4, sections)),
            dma((4, sections)),
        ],
        compiler_params=pltpu.CompilerParams(
            collective_id=0, has_side_effects=True, vmem_limit_bytes=60 * 1024 * 1024
        ),
    )(
        patches,
        clip_slot.reshape(1, -1),
        w_qkv,
        w_out,
        w_up,
        w_down,
        norm_gains,
        level_one_weight,
        level_two_weight,
        head_weight.T,
    )
    head_one, head_two = pl.pallas_call(
        split_heads,
        out_shape=(
            jax.ShapeDtypeStruct((outputs, one_rows), F32),
            jax.ShapeDtypeStruct((two_rows, outputs), F32),
        ),
        in_specs=[vmem],
        out_specs=(vmem, vmem),
    )(pltpu.with_memory_space_constraint(heads, pltpu.VMEM))
    return head_one.T, head_two


def solution(mesh):
    return jax.shard_map(
        on_device,
        mesh=mesh,
        in_specs=(
            P(("groups", "dp"), "section"),
            P("groups"),
            P("section", None, None),
            P("section", None, None),
            P("section", None, None),
            P("section", None, None),
            P("section", None, None),
            P(None, "section", None),
            P(None, "section", None),
            P("section", None),
        ),
        out_specs=(P(("groups", "dp"), None), P(("groups", "dp"), None)),
        check_vma=False,
    )
```

```python
import functools

import jax
import jax.numpy as jnp
from jax import lax
from jax.experimental import pallas as pl
from jax.experimental.pallas import tpu as pltpu
from jax.sharding import PartitionSpec as P

HEADS = 8
HEAD = 64
PATCHES = 16
TUB_CLIP = 2
EPSILON = 1e-05
UNIT_ROWS = 128
ROW_BLOCK = 128
CHUNK = 512
COLUMNS = 256
MESH = pl.DeviceIdType.MESH
F32 = jnp.float32
BF16 = jnp.bfloat16


def dot(a, b):
    return jnp.dot(a, b, preferred_element_type=F32)


def dot_nt(a, b):
    return lax.dot_general(a, b, (((1,), (1,)), ((), ())), preferred_element_type=F32)


def gelu(values):
    return jax.nn.gelu(values, approximate=True)


def gelu_rounded(values):
    x = values.astype(BF16)
    inner = x * (x * x * 0.035677408136300125 + 0.7978845608028654)
    return x * (jnp.tanh(inner) * 0.5 + 0.5)


def iota(shape, dim):
    return lax.broadcasted_iota(jnp.int32, shape, dim)


def centre(values, scaling):
    width = values.shape[1]

    def row_mean(parts):
        sums = parts[0]
        for part in parts[1:]:
            sums = sums + part
        return jnp.sum(sums, axis=-1, keepdims=True) * (1.0 / width)

    average = row_mean([values[:, start : start + 128] for start in range(0, width, 128)])
    centred = values - average
    squares = centred * centred
    spread = row_mean([squares[:, start : start + 128] for start in range(0, width, 128)]) + EPSILON
    return (centred * scaling).astype(BF16), spread


def backbone_layer(stream, gains, v_qkv, v_out, v_up, averaging, own, clip_mask, emit):
    inner = v_out.shape[0]
    hidden = v_up.shape[1]
    pair = 2 * HEAD
    group = averaging.shape[0]
    normed, spread = centre(stream, gains[0, 0:1])
    raw = []
    for start in range(0, inner, group):
        raw.append(
            (
                dot(normed, v_qkv[:, start : start + group]),
                dot(normed, v_qkv[:, inner + start : inner + start + group]),
            )
        )
    floor = EPSILON * spread

    def head_scale(part):
        return part * lax.rsqrt(dot((part * part).astype(BF16), averaging[...]) + floor)

    scaled = [
        ((head_scale(raw_q) * HEAD**-0.5).astype(BF16), head_scale(raw_k).astype(BF16))
        for raw_q, raw_k in raw
    ]
    scale = lax.rsqrt(spread)
    values = [
        (dot(normed, v_qkv[:, 2 * inner + start : 2 * inner + start + group]) * scale).astype(BF16)
        for start in range(0, inner, group)
    ]
    scores = []
    stacked = []
    for (query, key), value in zip(scaled, values):
        for lane in range(0, group, pair):
            k = key[:, lane : lane + pair]
            v = value[:, lane : lane + pair]
            k2 = jnp.concatenate([k, k], axis=0) * own[...]
            v2 = jnp.concatenate([v, v], axis=0) * own[...]
            scores.append(dot_nt(query[:, lane : lane + pair], k2))
            stacked.append(jnp.concatenate([v2, own[...]], axis=1))
    weights = [jnp.exp(score).astype(BF16) * clip_mask[...] for score in scores]
    mixed = []
    for weight, stack in zip(weights, stacked):
        both = dot(weight, stack)
        mixed.append((both[:, :pair] / both[:, pair:]).astype(BF16))
    residual = stream + dot(jnp.concatenate(mixed, axis=1), v_out[...])
    normed_b, spread_b = centre(residual, gains[0, 1:2])
    scale_b = lax.rsqrt(spread_b)
    parts = [
        gelu_rounded(dot(normed_b, v_up[:, start : start + CHUNK]) * scale_b)
        for start in range(0, hidden, CHUNK)
    ]
    emit(residual, jnp.concatenate(parts, axis=1))


def kernel(
    sections,
    shards,
    patches,
    slot_in,
    w_qkv,
    w_out,
    w_up,
    w_down,
    gains_in,
    one_weight,
    two_weight,
    head_in,
    heads,
    v_qkv,
    v_out,
    v_up,
    v_down,
    v_one,
    v_two,
    patch_buf,
    inbuf,
    outbuf,
    pooled_out,
    film_in,
    one_out,
    one_in,
    two_out,
    two_in,
    part_out,
    part_in,
    own_head,
    all_head,
    averaging,
    own,
    clip_mask,
    selector,
    clip_slot,
    gains,
    head_weight,
    weight_sem,
    gather_send,
    arrive,
    hop_send,
    film_send,
    film_recv,
    ex_send,
    ex_recv,
):
    section = lax.axis_index("section")
    shard = lax.axis_index("dp")
    last = sections - 1
    units, _, unit_rows, channels = outbuf.shape
    width = sections * channels
    tubes_unit = unit_rows // PATCHES
    outputs = head_weight.shape[0]
    barrier = pltpu.get_barrier_semaphore()
    for ds in range(sections):
        for dd in range(shards):
            if ds or dd:
                pl.semaphore_signal(
                    barrier,
                    inc=1,
                    device_id={
                        "section": lax.rem(section + ds, sections),
                        "dp": lax.rem(shard + dd, shards),
                    },
                    device_id_type=MESH,
                )
    loads = [
        pltpu.make_async_copy(source, target, weight_sem.at[index])
        for index, (source, target) in enumerate(
            (
                (w_qkv.at[0], v_qkv),
                (w_out.at[0], v_out),
                (w_up.at[0], v_up),
                (w_down.at[0], v_down),
                (one_weight, v_one),
                (two_weight, v_two),
            )
        )
    ]
    def each_unit(body):
        def step(u, carry):
            body(u)
            return carry

        lax.fori_loop(0, units, step, 0)

    def patch_rows(u):
        return pl.ds(pl.multiple_of(u * unit_rows, unit_rows), unit_rows)

    patch_load = pltpu.make_async_copy(patches, patch_buf, weight_sem.at[6])

    @pl.when(section > 0)
    def _():
        patch_load.start()

    @pl.when(section == 0)
    def _():
        each_unit(
            lambda u: pltpu.make_async_copy(
                patches.at[patch_rows(u)], inbuf.at[u, 0], arrive.at[u]
            ).start()
        )

    small = [
        pltpu.make_async_copy(source, target, weight_sem.at[7 + index])
        for index, (source, target) in enumerate(
            ((slot_in, clip_slot), (gains_in, gains), (head_in, head_weight))
        )
    ]
    for load in small + loads[:4]:
        load.start()

    same = iota(averaging.shape, 0) // HEAD == iota(averaging.shape, 1) // HEAD
    averaging[...] = jnp.where(same, 1.0 / HEAD, 0.0).astype(BF16)
    mine = (iota(own.shape, 0) < unit_rows) == (iota(own.shape, 1) < HEAD)
    own[...] = jnp.where(mine, 1.0, 0.0).astype(BF16)
    clip = PATCHES * TUB_CLIP
    same_clip = iota(clip_mask.shape, 0) // clip == iota(clip_mask.shape, 1) % unit_rows // clip
    clip_mask[...] = jnp.where(same_clip, 1.0, 0.0).astype(BF16)

    pl.semaphore_wait(barrier, sections * shards - 1)

    def patch_copy(u):
        return pltpu.make_async_remote_copy(
            src_ref=patch_buf.at[patch_rows(u)],
            dst_ref=inbuf.at[u, section],
            send_sem=gather_send.at[u],
            recv_sem=arrive.at[u],
            device_id={"section": 0},
            device_id_type=MESH,
        )

    @pl.when(section > 0)
    def _():
        patch_load.wait()
        each_unit(lambda u: patch_copy(u).start())

    def hop(u):
        return pltpu.make_async_remote_copy(
            src_ref=outbuf.at[u],
            dst_ref=inbuf.at[u],
            send_sem=hop_send.at[u],
            recv_sem=arrive.at[u],
            device_id={"section": lax.rem(section + 1, sections)},
            device_id_type=MESH,
        )

    def arrival(slot):
        return pltpu.make_async_copy(inbuf.at[slot], inbuf.at[slot], arrive.at[slot])

    tubes_own = units * tubes_unit
    tubes_pair = 2 * tubes_unit
    batches = ((0, tubes_own - tubes_pair), (tubes_own - tubes_pair, tubes_pair))
    film_targets = [
        (target, step)
        for target in range(sections)
        for step in range(shards)
        if not (target == last and step == 0)
    ]

    def film_copy(batch, target, step):
        start, count = batches[batch]
        return pltpu.make_async_remote_copy(
            src_ref=pooled_out.at[target, pl.ds(start, count)],
            dst_ref=film_in.at[shard, pl.ds(start, count)],
            send_sem=film_send.at[batch, target, step],
            recv_sem=film_recv.at[batch, shard],
            device_id={"section": target, "dp": lax.rem(shard + step, shards)},
            device_id_type=MESH,
        )

    def film_arrival(batch, source):
        start, count = batches[batch]
        return pltpu.make_async_copy(
            film_in.at[source, pl.ds(start, count)],
            film_in.at[source, pl.ds(start, count)],
            film_recv.at[batch, source],
        )

    pooling_shape = (tubes_pair, 2 * unit_rows)
    pooling = jnp.where(
        iota(pooling_shape, 1) // PATCHES == iota(pooling_shape, 0), 1.0 / PATCHES, 0.0
    ).astype(BF16)

    def pool(p, send=None):
        rows = pl.ds(pl.multiple_of(p * tubes_pair, tubes_pair), tubes_pair)
        for target in range(sections):
            both = jnp.concatenate([outbuf[2 * p, target], outbuf[2 * p + 1, target]], axis=0)
            pooled = dot(pooling, both).astype(BF16)
            pooled_out[target, rows] = pooled
            if target == last:
                film_in[shard, rows] = pooled
            if send is not None:
                send(target)

    def exchange(stage, outgoing, incoming, fill=None):
        copies = []
        for step in range(sections - 1, 0, -1):
            if fill is not None:
                fill(step)
            target = lax.rem(section + step, sections)
            copies.append(
                pltpu.make_async_remote_copy(
                    src_ref=outgoing(target),
                    dst_ref=incoming.at[section],
                    send_sem=ex_send.at[stage, step],
                    recv_sem=ex_recv.at[stage, section],
                    device_id={"section": target},
                    device_id_type=MESH,
                )
            )
            copies[-1].start()

        def arrivals():
            for step in range(1, sections):
                source = lax.rem(section + step, sections)
                pltpu.make_async_copy(
                    incoming.at[source], incoming.at[source], ex_recv.at[stage, source]
                ).wait()

        def sent():
            for copy in copies:
                copy.wait_send()

        return arrivals, sent

    for load in small:
        load.wait()
    own_head[...] = jnp.zeros(own_head.shape, BF16)
    own_head[0:outputs] = head_weight[...]
    head_arrivals, head_sent = exchange(3, lambda target: own_head, all_head)
    all_head[section] = own_head[...]

    tubes = selector.shape[1]
    clips = tubes // TUB_CLIP
    spread_shape = (clips, tubes)
    spread = jnp.where(iota(spread_shape, 1) // TUB_CLIP == iota(spread_shape, 0), 1.0, 0.0)
    slots = jnp.broadcast_to(clip_slot[...].astype(F32), (8, clips)).astype(BF16)
    position = TUB_CLIP * dot(slots, spread.astype(BF16))[0:1]
    position = position + (iota((1, tubes), 1) % TUB_CLIP).astype(F32)
    two_rows = two_out.shape[0]
    one_rows = 3 * two_rows
    row = iota((one_rows, 1), 0)
    level_index = 2 * (shard * two_rows + row % two_rows) + row // two_rows - 1
    for tap in range(3):
        wanted = (2 * level_index + tap - 1).astype(F32)
        chosen = jnp.where(position == wanted, 1.0, 0.0).astype(BF16)
        selector[tap * one_rows : (tap + 1) * one_rows] = chosen

    for load in loads[:4]:
        load.wait()
    for load in loads[4:]:
        load.start()

    blocks = max(1, COLUMNS // channels)

    def run_unit(u):
        arrival(u).wait()
        stream = jnp.concatenate([inbuf[u, source] for source in range(sections)], axis=1)

        def emit(residual, gated):
            for first in range(0, sections, blocks):
                columns = slice(first * channels, (first + blocks) * channels)
                result = (residual[:, columns] + dot(gated, v_down[:, columns])).astype(BF16)
                for block in range(blocks):
                    outbuf[u, first + block] = result[:, block * channels : (block + 1) * channels]

        backbone_layer(
            stream.astype(F32), gains, v_qkv, v_out, v_up, averaging, own, clip_mask, emit
        )

        @pl.when(section < last)
        def _():
            hop(u).start()

        def film_start(batch, chosen):
            for target, step in film_targets:
                if target == chosen:
                    film_copy(batch, target, step).start()

        @pl.when((section == last) & (u % 2 == 1) & (u < units - 1))
        def _():
            pool(u // 2)

            @pl.when(u == units - 3)
            def _():
                for target in range(sections):
                    film_start(0, target)

        @pl.when((section == last) & (u == units - 1))
        def _():
            pool(u // 2, lambda target: film_start(1, target))

    each_unit(run_unit)

    def film_sent(batch):
        @pl.when(section == last)
        def _():
            for target, step in film_targets:
                film_copy(batch, target, step).wait_send()

    def finish():
        head_arrivals()
        head_sent()

        @pl.when(section > 0)
        def _():
            each_unit(lambda u: patch_copy(u).wait_send())

        @pl.when(section < last)
        def _():
            each_unit(lambda u: hop(u).wait_send())

        film_sent(0)

    loads[4].wait()
    loads[5].wait()
    finish()

    for batch in (0, 1):

        @pl.when(section < last)
        def _():
            film_arrival(batch, shard).wait()

        for step in range(1, shards):
            film_arrival(batch, lax.rem(shard + step, shards)).wait()

    pooled = film_in[...].reshape(tubes, channels)
    picked = dot(selector[...], pooled).astype(BF16)
    taps = [picked[tap * one_rows : (tap + 1) * one_rows] for tap in range(3)]

    def conv(parts, weight, columns=slice(None)):
        total = dot(parts[0], weight[0, :, columns])
        for tap in (1, 2):
            total = total + dot(parts[tap], weight[tap, :, columns])
        return total.astype(BF16)

    def total(incoming):
        value = incoming[0].astype(F32)
        for source in range(1, sections):
            value = value + incoming[source].astype(F32)
        return value

    if channels % 128 == 0:

        def fill(step):
            target = lax.rem(section + step, sections)
            columns = pl.ds(pl.multiple_of(target * channels, channels), channels)
            one_out[target] = conv(taps, v_one, columns)

    else:
        partial = conv(taps, v_one)
        for target in range(sections):
            one_out[target] = partial[:, target * channels : (target + 1) * channels]

        def fill(step):
            pass

    arrivals, one_sent = exchange(0, lambda target: one_out.at[target], one_in, fill)
    fill(0)
    one_in[section] = one_out[section]
    arrivals()
    one = gelu(total(one_in)).astype(BF16)

    two_out[...] = conv([one[block * two_rows : (block + 1) * two_rows] for block in range(3)], v_two)
    two_arrivals, two_sent = exchange(1, lambda target: two_out, two_in)
    natural = 2 * two_rows
    order = (natural, one_rows)
    chosen = iota(order, 1) == (1 + iota(order, 0) % 2) * two_rows + iota(order, 0) // 2
    one_natural = dot(jnp.where(chosen, 1.0, 0.0).astype(BF16), one).astype(BF16)
    part_out[...] = dot_nt(own_head[...], one_natural)[0 : part_out.shape[0]]
    part_arrivals, part_sent = exchange(2, lambda target: part_out, part_in)
    two_in[section] = two_out[...]
    part_in[section] = part_out[...]
    one_sent()
    film_sent(1)
    two_arrivals()
    two = gelu(total(two_in)).astype(BF16)
    every_head = jnp.concatenate([all_head[source] for source in range(sections)], axis=1)
    level_two = dot_nt(two, every_head)
    part_arrivals()
    heads[0 : part_out.shape[0], 0:natural] = total(part_in)
    heads[own_head.shape[0] :, 0 : own_head.shape[0]] = level_two
    two_sent()
    part_sent()


def split_heads(heads, head_one, head_two):
    outputs, natural = head_one.shape
    two_rows = head_two.shape[0]
    head_one[...] = heads[0:outputs, 0:natural]
    head_two[...] = heads[heads.shape[0] - two_rows :, 0:outputs]


def on_device(
    patches,
    clip_slot,
    w_qkv,
    w_out,
    w_up,
    w_down,
    norm_gains,
    level_one_weight,
    level_two_weight,
    head_weight,
):
    sections = lax.axis_size("section")
    shards = lax.axis_size("dp")
    rows, channels = patches.shape
    width = channels * sections
    unit_rows = UNIT_ROWS
    units = rows // unit_rows
    tubes_unit = unit_rows // PATCHES
    outputs = head_weight.shape[1]
    one_rows = rows // PATCHES // 2
    two_rows = one_rows // 2
    vmem = pl.BlockSpec(memory_space=pltpu.VMEM)
    anywhere = pl.BlockSpec(memory_space=pl.ANY)
    dma = pltpu.SemaphoreType.DMA
    group = min(256, w_out.shape[1])
    part_rows = -(-outputs // 8) * 8
    head_rows = -(-outputs // 16) * 16
    heads = pl.pallas_call(
        functools.partial(kernel, sections, shards),
        out_shape=pltpu.VMEM((head_rows + two_rows, 128), F32),
        in_specs=[anywhere] * 10,
        out_specs=vmem,
        scratch_shapes=[
            pltpu.VMEM(w_qkv.shape[1:], BF16),
            pltpu.VMEM(w_out.shape[1:], BF16),
            pltpu.VMEM(w_up.shape[1:], BF16),
            pltpu.VMEM(w_down.shape[1:], BF16),
            pltpu.VMEM(level_one_weight.shape, BF16),
            pltpu.VMEM(level_two_weight.shape, BF16),
            pltpu.VMEM(patches.shape, BF16),
            pltpu.VMEM((units, sections, unit_rows, channels), BF16),
            pltpu.VMEM((units, sections, unit_rows, channels), BF16),
            pltpu.VMEM((sections, units * tubes_unit, channels), BF16),
            pltpu.VMEM((shards, units * tubes_unit, channels), BF16),
            pltpu.VMEM((sections, 3 * two_rows, channels), BF16),
            pltpu.VMEM((sections, 3 * two_rows, channels), BF16),
            pltpu.VMEM((two_rows, width), BF16),
            pltpu.VMEM((sections, two_rows, width), BF16),
            pltpu.VMEM((part_rows, 2 * two_rows), F32),
            pltpu.VMEM((sections, part_rows, 2 * two_rows), F32),
            pltpu.VMEM((head_rows, channels), BF16),
            pltpu.VMEM((sections, head_rows, channels), BF16),
            pltpu.VMEM((group, group), BF16),
            pltpu.VMEM((2 * unit_rows, 2 * HEAD), BF16),
            pltpu.VMEM((unit_rows, 2 * unit_rows), BF16),
            pltpu.VMEM((9 * two_rows, shards * units * tubes_unit), BF16),
            pltpu.VMEM((1, clip_slot.shape[0]), jnp.int32),
            pltpu.VMEM(norm_gains.shape, F32),
            pltpu.VMEM((outputs, channels), BF16),
            dma((10,)),
            dma((units,)),
            dma((units,)),
            dma((units,)),
            dma((2, sections, shards)),
            dma((2, shards)),
            dma((4, sections)),
            dma((4, sections)),
        ],
        compiler_params=pltpu.CompilerParams(
            collective_id=0, has_side_effects=True, vmem_limit_bytes=60 * 1024 * 1024
        ),
    )(
        patches,
        clip_slot.reshape(1, -1),
        w_qkv,
        w_out,
        w_up,
        w_down,
        norm_gains,
        level_one_weight,
        level_two_weight,
        head_weight.T,
    )
    head_one, head_two = pl.pallas_call(
        split_heads,
        out_shape=(
            jax.ShapeDtypeStruct((outputs, one_rows), F32),
            jax.ShapeDtypeStruct((two_rows, outputs), F32),
        ),
        in_specs=[vmem],
        out_specs=(vmem, vmem),
    )(pltpu.with_memory_space_constraint(heads, pltpu.VMEM))
    return head_one.T, head_two


def solution(mesh):
    return jax.shard_map(
        on_device,
        mesh=mesh,
        in_specs=(
            P(("groups", "dp"), "section"),
            P("groups"),
            P("section", None, None),
            P("section", None, None),
            P("section", None, None),
            P("section", None, None),
            P("section", None, None),
            P(None, "section", None),
            P(None, "section", None),
            P("section", None),
        ),
        out_specs=(P(("groups", "dp"), None), P(("groups", "dp"), None)),
        check_vma=False,
    )
```

```python
import functools

import jax
import jax.numpy as jnp
from jax import lax
from jax.experimental import pallas as pl
from jax.experimental.pallas import tpu as pltpu
from jax.sharding import PartitionSpec as P

HEADS = 8
HEAD = 64
PATCHES = 16
TUB_CLIP = 2
EPSILON = 1e-05
UNIT_ROWS = 128
ROW_BLOCK = 128
CHUNK = 512
COLUMNS = 256
MESH = pl.DeviceIdType.MESH
F32 = jnp.float32
BF16 = jnp.bfloat16


def dot(a, b):
    return jnp.dot(a, b, preferred_element_type=F32)


def dot_nt(a, b):
    return lax.dot_general(a, b, (((1,), (1,)), ((), ())), preferred_element_type=F32)


def gelu(values):
    return jax.nn.gelu(values, approximate=True)


def gelu_rounded(values):
    x = values.astype(BF16)
    inner = x * (x * x * 0.035677408136300125 + 0.7978845608028654)
    return x * (jnp.tanh(inner) * 0.5 + 0.5)


def iota(shape, dim):
    return lax.broadcasted_iota(jnp.int32, shape, dim)


def centre(values, scaling):
    width = values.shape[1]
    lanes = [values[:, start : start + 128] for start in range(0, width, 128)]
    sums = lanes[0]
    squares = lanes[0] * lanes[0]
    for lane in lanes[1:]:
        sums = sums + lane
        squares = squares + lane * lane
    average = jnp.sum(sums, axis=-1, keepdims=True) * (1.0 / width)
    square = jnp.sum(squares, axis=-1, keepdims=True) * (1.0 / width)
    spread = jnp.maximum(square - average * average, 0.0) + EPSILON
    return ((values - average) * scaling).astype(BF16), spread


def backbone_layer(stream, gains, v_qkv, v_out, v_up, averaging, own, clip_mask, emit):
    inner = v_out.shape[0]
    hidden = v_up.shape[1]
    pair = 2 * HEAD
    group = averaging.shape[0]
    normed, spread = centre(stream, gains[0, 0:1])
    raw = []
    for start in range(0, inner, group):
        raw.append(
            (
                dot(normed, v_qkv[:, start : start + group]),
                dot(normed, v_qkv[:, inner + start : inner + start + group]),
            )
        )
    floor = EPSILON * spread

    def head_scale(part):
        return part * lax.rsqrt(dot((part * part).astype(BF16), averaging[...]) + floor)

    scaled = [
        ((head_scale(raw_q) * HEAD**-0.5).astype(BF16), head_scale(raw_k).astype(BF16))
        for raw_q, raw_k in raw
    ]
    scale = lax.rsqrt(spread)
    values = [
        (dot(normed, v_qkv[:, 2 * inner + start : 2 * inner + start + group]) * scale).astype(BF16)
        for start in range(0, inner, group)
    ]
    scores = []
    stacked = []
    for (query, key), value in zip(scaled, values):
        for lane in range(0, group, pair):
            k = key[:, lane : lane + pair]
            v = value[:, lane : lane + pair]
            k2 = jnp.concatenate([k, k], axis=0) * own[...]
            v2 = jnp.concatenate([v, v], axis=0) * own[...]
            scores.append(dot_nt(query[:, lane : lane + pair], k2))
            stacked.append(jnp.concatenate([v2, own[...]], axis=1))
    weights = [jnp.exp(score).astype(BF16) * clip_mask[...] for score in scores]
    mixed = []
    for weight, stack in zip(weights, stacked):
        both = dot(weight, stack)
        mixed.append((both[:, :pair] / both[:, pair:]).astype(BF16))
    residual = stream + dot(jnp.concatenate(mixed, axis=1), v_out[...])
    normed_b, spread_b = centre(residual, gains[0, 1:2])
    scale_b = lax.rsqrt(spread_b)
    parts = [
        gelu_rounded(dot(normed_b, v_up[:, start : start + CHUNK]) * scale_b)
        for start in range(0, hidden, CHUNK)
    ]
    emit(residual, jnp.concatenate(parts, axis=1))


def kernel(
    sections,
    shards,
    patches,
    slot_in,
    w_qkv,
    w_out,
    w_up,
    w_down,
    gains_in,
    one_weight,
    two_weight,
    head_in,
    heads,
    v_qkv,
    v_out,
    v_up,
    v_down,
    v_one,
    v_two,
    patch_buf,
    inbuf,
    outbuf,
    pooled_out,
    film_in,
    one_out,
    one_in,
    two_out,
    two_in,
    part_out,
    part_in,
    own_head,
    all_head,
    averaging,
    own,
    clip_mask,
    selector,
    clip_slot,
    gains,
    head_weight,
    weight_sem,
    gather_send,
    arrive,
    hop_send,
    film_send,
    film_recv,
    ex_send,
    ex_recv,
    ready,
):
    section = lax.axis_index("section")
    shard = lax.axis_index("dp")
    last = sections - 1
    units, _, unit_rows, channels = outbuf.shape
    width = sections * channels
    tubes_unit = unit_rows // PATCHES
    outputs = head_weight.shape[0]
    barrier = pltpu.get_barrier_semaphore()
    def greet(target, where):
        pl.semaphore_signal(
            target,
            inc=1,
            device_id={"section": where[0], "dp": where[1]},
            device_id_type=MESH,
        )

    for ds in range(1, sections):
        greet(barrier, (lax.rem(section + ds, sections), shard))

    @pl.when(section == last)
    def _():
        for dd in range(1, shards):
            greet(barrier, (0, lax.rem(shard + dd, shards)))

    loads = [
        pltpu.make_async_copy(source, target, weight_sem.at[index])
        for index, (source, target) in enumerate(
            (
                (w_qkv.at[0], v_qkv),
                (w_out.at[0], v_out),
                (w_up.at[0], v_up),
                (w_down.at[0], v_down),
                (one_weight, v_one),
                (two_weight, v_two),
            )
        )
    ]
    def each_unit(body):
        def step(u, carry):
            body(u)
            return carry

        lax.fori_loop(0, units, step, 0)

    def patch_rows(u):
        return pl.ds(pl.multiple_of(u * unit_rows, unit_rows), unit_rows)

    patch_load = pltpu.make_async_copy(patches, patch_buf, weight_sem.at[6])

    @pl.when(section > 0)
    def _():
        patch_load.start()

    @pl.when(section == 0)
    def _():
        each_unit(
            lambda u: pltpu.make_async_copy(
                patches.at[patch_rows(u)], inbuf.at[u, 0], arrive.at[u]
            ).start()
        )

    small = [
        pltpu.make_async_copy(source, target, weight_sem.at[7 + index])
        for index, (source, target) in enumerate(
            ((slot_in, clip_slot), (gains_in, gains), (head_in, head_weight))
        )
    ]
    for load in small + loads[:4]:
        load.start()

    same = iota(averaging.shape, 0) // HEAD == iota(averaging.shape, 1) // HEAD
    averaging[...] = jnp.where(same, 1.0 / HEAD, 0.0).astype(BF16)
    mine = (iota(own.shape, 0) < unit_rows) == (iota(own.shape, 1) < HEAD)
    own[...] = jnp.where(mine, 1.0, 0.0).astype(BF16)
    clip = PATCHES * TUB_CLIP
    same_clip = iota(clip_mask.shape, 0) // clip == iota(clip_mask.shape, 1) % unit_rows // clip
    clip_mask[...] = jnp.where(same_clip, 1.0, 0.0).astype(BF16)

    @pl.when(section == 0)
    def _():
        pl.semaphore_wait(barrier, sections + shards - 2)
        for dd in range(shards):
            greet(ready, (last, lax.rem(shard + dd, shards)))

    @pl.when(section > 0)
    def _():
        pl.semaphore_wait(barrier, sections - 1)


    def patch_copy(u):
        return pltpu.make_async_remote_copy(
            src_ref=patch_buf.at[patch_rows(u)],
            dst_ref=inbuf.at[u, section],
            send_sem=gather_send.at[u],
            recv_sem=arrive.at[u],
            device_id={"section": 0},
            device_id_type=MESH,
        )

    @pl.when(section > 0)
    def _():
        patch_load.wait()
        each_unit(lambda u: patch_copy(u).start())

    def hop(u):
        return pltpu.make_async_remote_copy(
            src_ref=outbuf.at[u],
            dst_ref=inbuf.at[u],
            send_sem=hop_send.at[u],
            recv_sem=arrive.at[u],
            device_id={"section": lax.rem(section + 1, sections)},
            device_id_type=MESH,
        )

    def arrival(slot):
        return pltpu.make_async_copy(inbuf.at[slot], inbuf.at[slot], arrive.at[slot])

    tubes_own = units * tubes_unit
    tubes_pair = 2 * tubes_unit
    batches = ((0, tubes_own - tubes_pair), (tubes_own - tubes_pair, tubes_pair))
    film_targets = [
        (target, step)
        for target in range(sections)
        for step in range(shards)
        if not (target == last and step == 0)
    ]

    def film_copy(batch, target, step):
        start, count = batches[batch]
        return pltpu.make_async_remote_copy(
            src_ref=pooled_out.at[target, pl.ds(start, count)],
            dst_ref=film_in.at[shard, pl.ds(start, count)],
            send_sem=film_send.at[batch, target, step],
            recv_sem=film_recv.at[batch, shard],
            device_id={"section": target, "dp": lax.rem(shard + step, shards)},
            device_id_type=MESH,
        )

    def film_arrival(batch, source):
        start, count = batches[batch]
        return pltpu.make_async_copy(
            film_in.at[source, pl.ds(start, count)],
            film_in.at[source, pl.ds(start, count)],
            film_recv.at[batch, source],
        )

    pooling_shape = (tubes_pair, 2 * unit_rows)
    pooling = jnp.where(
        iota(pooling_shape, 1) // PATCHES == iota(pooling_shape, 0), 1.0 / PATCHES, 0.0
    ).astype(BF16)

    def pool(p, send=None):
        rows = pl.ds(pl.multiple_of(p * tubes_pair, tubes_pair), tubes_pair)
        for target in range(sections):
            both = jnp.concatenate([outbuf[2 * p, target], outbuf[2 * p + 1, target]], axis=0)
            pooled = dot(pooling, both).astype(BF16)
            pooled_out[target, rows] = pooled
            if target == last:
                film_in[shard, rows] = pooled
            if send is not None:
                send(target)

    def exchange(stage, outgoing, incoming, fill=None):
        copies = []
        for step in range(sections - 1, 0, -1):
            if fill is not None:
                fill(step)
            target = lax.rem(section + step, sections)
            copies.append(
                pltpu.make_async_remote_copy(
                    src_ref=outgoing(target),
                    dst_ref=incoming.at[section],
                    send_sem=ex_send.at[stage, step],
                    recv_sem=ex_recv.at[stage, section],
                    device_id={"section": target},
                    device_id_type=MESH,
                )
            )
            copies[-1].start()

        def arrivals():
            for step in range(1, sections):
                source = lax.rem(section + step, sections)
                pltpu.make_async_copy(
                    incoming.at[source], incoming.at[source], ex_recv.at[stage, source]
                ).wait()

        def sent():
            for copy in copies:
                copy.wait_send()

        return arrivals, sent

    for load in small:
        load.wait()
    own_head[...] = jnp.zeros(own_head.shape, BF16)
    own_head[0:outputs] = head_weight[...]
    head_arrivals, head_sent = exchange(3, lambda target: own_head, all_head)
    all_head[section] = own_head[...]

    tubes = selector.shape[1]
    clips = tubes // TUB_CLIP
    spread_shape = (clips, tubes)
    spread = jnp.where(iota(spread_shape, 1) // TUB_CLIP == iota(spread_shape, 0), 1.0, 0.0)
    slots = jnp.broadcast_to(clip_slot[...].astype(F32), (8, clips)).astype(BF16)
    position = TUB_CLIP * dot(slots, spread.astype(BF16))[0:1]
    position = position + (iota((1, tubes), 1) % TUB_CLIP).astype(F32)
    two_rows = two_out.shape[0]
    one_rows = 3 * two_rows
    row = iota((one_rows, 1), 0)
    level_index = 2 * (shard * two_rows + row % two_rows) + row // two_rows - 1
    for tap in range(3):
        wanted = (2 * level_index + tap - 1).astype(F32)
        chosen = jnp.where(position == wanted, 1.0, 0.0).astype(BF16)
        selector[tap * one_rows : (tap + 1) * one_rows] = chosen

    @pl.when(section == last)
    def _():
        pl.semaphore_wait(ready, shards)

    for load in loads[:4]:
        load.wait()
    for load in loads[4:]:
        load.start()

    blocks = max(1, COLUMNS // channels)

    def run_unit(u):
        arrival(u).wait()
        stream = jnp.concatenate([inbuf[u, source] for source in range(sections)], axis=1)

        def emit(residual, gated):
            for first in range(0, sections, blocks):
                columns = slice(first * channels, (first + blocks) * channels)
                result = (residual[:, columns] + dot(gated, v_down[:, columns])).astype(BF16)
                for block in range(blocks):
                    outbuf[u, first + block] = result[:, block * channels : (block + 1) * channels]

        backbone_layer(
            stream.astype(F32), gains, v_qkv, v_out, v_up, averaging, own, clip_mask, emit
        )

        @pl.when(section < last)
        def _():
            hop(u).start()

        def film_start(batch, chosen):
            for target, step in film_targets:
                if target == chosen:
                    film_copy(batch, target, step).start()

        @pl.when((section == last) & (u % 2 == 1) & (u < units - 1))
        def _():
            pool(u // 2)

            @pl.when(u == units - 3)
            def _():
                for target in range(sections):
                    film_start(0, target)

        @pl.when((section == last) & (u == units - 1))
        def _():
            pool(u // 2, lambda target: film_start(1, target))

    each_unit(run_unit)

    def film_sent(batch):
        @pl.when(section == last)
        def _():
            for target, step in film_targets:
                film_copy(batch, target, step).wait_send()

    def finish():
        head_arrivals()
        head_sent()

        @pl.when(section > 0)
        def _():
            each_unit(lambda u: patch_copy(u).wait_send())

        @pl.when(section < last)
        def _():
            each_unit(lambda u: hop(u).wait_send())

        film_sent(0)

    loads[4].wait()
    loads[5].wait()
    finish()

    for batch in (0, 1):

        @pl.when(section < last)
        def _():
            film_arrival(batch, shard).wait()

        for step in range(1, shards):
            film_arrival(batch, lax.rem(shard + step, shards)).wait()

    pooled = film_in[...].reshape(tubes, channels)
    picked = dot(selector[...], pooled).astype(BF16)
    taps = [picked[tap * one_rows : (tap + 1) * one_rows] for tap in range(3)]

    def conv(parts, weight, columns=slice(None)):
        total = dot(parts[0], weight[0, :, columns])
        for tap in (1, 2):
            total = total + dot(parts[tap], weight[tap, :, columns])
        return total.astype(BF16)

    def total(incoming):
        value = incoming[0].astype(F32)
        for source in range(1, sections):
            value = value + incoming[source].astype(F32)
        return value

    if channels % 128 == 0:

        def fill(step):
            target = lax.rem(section + step, sections)
            columns = pl.ds(pl.multiple_of(target * channels, channels), channels)
            one_out[target] = conv(taps, v_one, columns)

    else:
        partial = conv(taps, v_one)
        for target in range(sections):
            one_out[target] = partial[:, target * channels : (target + 1) * channels]

        def fill(step):
            pass

    arrivals, one_sent = exchange(0, lambda target: one_out.at[target], one_in, fill)
    fill(0)
    one_in[section] = one_out[section]
    arrivals()
    one = gelu(total(one_in)).astype(BF16)

    two_out[...] = conv([one[block * two_rows : (block + 1) * two_rows] for block in range(3)], v_two)
    two_arrivals, two_sent = exchange(1, lambda target: two_out, two_in)
    natural = 2 * two_rows
    order = (natural, one_rows)
    chosen = iota(order, 1) == (1 + iota(order, 0) % 2) * two_rows + iota(order, 0) // 2
    one_natural = dot(jnp.where(chosen, 1.0, 0.0).astype(BF16), one).astype(BF16)
    part_out[...] = dot_nt(own_head[...], one_natural)[0 : part_out.shape[0]]
    part_arrivals, part_sent = exchange(2, lambda target: part_out, part_in)
    two_in[section] = two_out[...]
    part_in[section] = part_out[...]
    one_sent()
    film_sent(1)
    two_arrivals()
    two = gelu(total(two_in)).astype(BF16)
    every_head = jnp.concatenate([all_head[source] for source in range(sections)], axis=1)
    level_two = dot_nt(two, every_head)
    part_arrivals()
    heads[0 : part_out.shape[0], 0:natural] = total(part_in)
    heads[own_head.shape[0] :, 0 : own_head.shape[0]] = level_two
    two_sent()
    part_sent()


def split_heads(heads, head_one, head_two):
    outputs, natural = head_one.shape
    two_rows = head_two.shape[0]
    head_one[...] = heads[0:outputs, 0:natural]
    head_two[...] = heads[heads.shape[0] - two_rows :, 0:outputs]


def on_device(
    patches,
    clip_slot,
    w_qkv,
    w_out,
    w_up,
    w_down,
    norm_gains,
    level_one_weight,
    level_two_weight,
    head_weight,
):
    sections = lax.axis_size("section")
    shards = lax.axis_size("dp")
    rows, channels = patches.shape
    width = channels * sections
    unit_rows = UNIT_ROWS
    units = rows // unit_rows
    tubes_unit = unit_rows // PATCHES
    outputs = head_weight.shape[1]
    one_rows = rows // PATCHES // 2
    two_rows = one_rows // 2
    vmem = pl.BlockSpec(memory_space=pltpu.VMEM)
    anywhere = pl.BlockSpec(memory_space=pl.ANY)
    dma = pltpu.SemaphoreType.DMA
    group = min(256, w_out.shape[1])
    part_rows = -(-outputs // 8) * 8
    head_rows = -(-outputs // 16) * 16
    heads = pl.pallas_call(
        functools.partial(kernel, sections, shards),
        out_shape=pltpu.VMEM((head_rows + two_rows, 128), F32),
        in_specs=[anywhere] * 10,
        out_specs=vmem,
        scratch_shapes=[
            pltpu.VMEM(w_qkv.shape[1:], BF16),
            pltpu.VMEM(w_out.shape[1:], BF16),
            pltpu.VMEM(w_up.shape[1:], BF16),
            pltpu.VMEM(w_down.shape[1:], BF16),
            pltpu.VMEM(level_one_weight.shape, BF16),
            pltpu.VMEM(level_two_weight.shape, BF16),
            pltpu.VMEM(patches.shape, BF16),
            pltpu.VMEM((units, sections, unit_rows, channels), BF16),
            pltpu.VMEM((units, sections, unit_rows, channels), BF16),
            pltpu.VMEM((sections, units * tubes_unit, channels), BF16),
            pltpu.VMEM((shards, units * tubes_unit, channels), BF16),
            pltpu.VMEM((sections, 3 * two_rows, channels), BF16),
            pltpu.VMEM((sections, 3 * two_rows, channels), BF16),
            pltpu.VMEM((two_rows, width), BF16),
            pltpu.VMEM((sections, two_rows, width), BF16),
            pltpu.VMEM((part_rows, 2 * two_rows), F32),
            pltpu.VMEM((sections, part_rows, 2 * two_rows), F32),
            pltpu.VMEM((head_rows, channels), BF16),
            pltpu.VMEM((sections, head_rows, channels), BF16),
            pltpu.VMEM((group, group), BF16),
            pltpu.VMEM((2 * unit_rows, 2 * HEAD), BF16),
            pltpu.VMEM((unit_rows, 2 * unit_rows), BF16),
            pltpu.VMEM((9 * two_rows, shards * units * tubes_unit), BF16),
            pltpu.VMEM((1, clip_slot.shape[0]), jnp.int32),
            pltpu.VMEM(norm_gains.shape, F32),
            pltpu.VMEM((outputs, channels), BF16),
            dma((10,)),
            dma((units,)),
            dma((units,)),
            dma((units,)),
            dma((2, sections, shards)),
            dma((2, shards)),
            dma((4, sections)),
            dma((4, sections)),
            pltpu.SemaphoreType.REGULAR,
        ],
        compiler_params=pltpu.CompilerParams(
            collective_id=0, has_side_effects=True, vmem_limit_bytes=60 * 1024 * 1024
        ),
    )(
        patches,
        clip_slot.reshape(1, -1),
        w_qkv,
        w_out,
        w_up,
        w_down,
        norm_gains,
        level_one_weight,
        level_two_weight,
        head_weight.T,
    )
    head_one, head_two = pl.pallas_call(
        split_heads,
        out_shape=(
            jax.ShapeDtypeStruct((outputs, one_rows), F32),
            jax.ShapeDtypeStruct((two_rows, outputs), F32),
        ),
        in_specs=[vmem],
        out_specs=(vmem, vmem),
    )(pltpu.with_memory_space_constraint(heads, pltpu.VMEM))
    return head_one.T, head_two


def solution(mesh):
    return jax.shard_map(
        on_device,
        mesh=mesh,
        in_specs=(
            P(("groups", "dp"), "section"),
            P("groups"),
            P("section", None, None),
            P("section", None, None),
            P("section", None, None),
            P("section", None, None),
            P("section", None, None),
            P(None, "section", None),
            P(None, "section", None),
            P("section", None),
        ),
        out_specs=(P(("groups", "dp"), None), P(("groups", "dp"), None)),
        check_vma=False,
    )
```
